1024 devices in a mesh: segment: 2 (over y_hi), fsdp: 32 (over z), seq: 16 (over y_lo, x, core).
Axes of the slice: x: 4, y: 4 (y_hi: 2, y_lo: 2; y = y_hi * 2 + y_lo), z: 32, core: 2. Of those that a mesh axis runs over, the one named last changes fastest.
Arguments:
- branch_x: bfloat16 [64, 2048, 4096], P(('segment', 'fsdp'), 'seq'), may hold values from -6 to 6
- positions: int32 [64, 2048], P(('segment', 'fsdp'), 'seq'), may hold values from 0 to 2047, as said below
- teacher_held: bfloat16 [64, 2048, 4096], P(('segment', 'fsdp'), 'seq'), may hold values from -6 to 6
- gate_weights: bfloat16 [32, 2, 128, 128], P('fsdp'), may hold values from -0.5 to 0.5
- gate_bias: float32 [2, 4096], replicated, may hold values from -4 to 4
- conv_weight: float32 [4, 4096], replicated, may hold values from -3 to 3
- conv_bias: float32 [4096], replicated, may hold values from -3 to 3
- decay_rate: float32 [4096], replicated, as said below
Outputs:
- student_out: bfloat16 [64, 2048, 4096], P(('segment', 'fsdp'), 'seq')
- token_loss: float32 [64, 2048], P(('segment', 'fsdp'), 'seq')
The draws below stay inside these ranges and needn't reach their ends.
Inputs may be any that keep to these rules, and one draw needn't show every extreme that they name: `positions`: within each sequence a token's position is 0 at a document start and one more than the previous token's position otherwise; every sequence begins with a document start; the first sequence is one whole document. `decay_rate`: rates are positive.
All inputs are finite; a program needn't handle non-finite values.
Results may differ from the reference program's by a relative error of at most 0.0055.
Values may be sent and summed in bfloat16 or wider, within the bound.
A program may use at most 64 MiB of HBM per device.

```python
import jax
import jax.numpy as jnp
from jax import lax

HEADS = 32
HS = 128
R = 4096
LEN = 2048
SEQS = 64


def draw_positions(key, part):
    starts = jax.random.randint(key, (SEQS, LEN), 0, LEN // 4) == 0
    index_row = jnp.arange(LEN, dtype=jnp.int32)[None, :] + jnp.zeros((SEQS, LEN), jnp.int32)
    seq_row = jnp.arange(SEQS, dtype=jnp.int32)[:, None] + jnp.zeros((SEQS, LEN), jnp.int32)
    starts = jnp.logical_and(starts, seq_row != 0)
    starts = jnp.logical_or(starts, index_row == 0)
    marks = jnp.where(starts, index_row, jnp.zeros_like(index_row))
    latest = lax.cummax(marks, axis=1)
    return (index_row - latest).astype(jnp.int32)


def draw_decay_rate(key, part):
    first_key = jax.random.fold_in(key, 11)
    lowest = jnp.log(jnp.float32(0.02))
    highest = jnp.log(jnp.float32(LEN) / 160.0)
    rates = jnp.exp(lowest + jax.random.uniform(first_key, (R,), jnp.float32) * (highest - lowest))
    return rates.astype(jnp.float32)


def block_scale(own_key, dims, pieces, smallest, top_value):
    def one(position, blocks):
        heights = jax.random.uniform(jax.random.fold_in(jax.random.fold_in(own_key, 6), position), (blocks,), jnp.float32, smallest / len(pieces), top_value / len(pieces))
        return jnp.repeat(jnp.exp(heights), dims[position] // blocks).reshape((-1,) + (1,) * (len(dims) - position - 1))

    level = one(*pieces[0])
    for cut in pieces[1:]:
        level = level * one(*cut)
    return level


def normal_values(rng, extent, deviation, reach, cuts=(), held_as=jnp.bfloat16):
    entries = jax.random.normal(rng, extent, jnp.float32) * deviation
    if len(cuts) > 0:
        entries = block_scale(rng, extent, cuts, -0.22, 0.18) * entries
    return jnp.clip(entries, min=-reach, max=reach).astype(held_as)


def setup_inputs(seed: int = 0) -> dict:
    key_list = jax.random.split(jax.random.key(seed), 9)
    branch_x = normal_values(key_list[0], (SEQS, LEN, R), 1.0, 6.0, ((0, 64), (1, 16)))
    positions = draw_positions(jax.random.fold_in(key_list[8], 71), 0)
    teacher_held = normal_values(key_list[2], (SEQS, LEN, R), 1.0, 6.0, ((0, 64), (1, 16)))
    gate_weights = normal_values(key_list[3], (HEADS, 2, HS, HS), HS ** -0.5, 0.5, ((0, 32),))
    gate_bias = normal_values(key_list[4], (2, R), 1.0, 4.0, (), jnp.float32)
    conv_weight = normal_values(key_list[5], (4, R), 4 ** -0.5, 3.0, (), jnp.float32)
    conv_bias = normal_values(key_list[6], (R,), 0.5, 3.0, (), jnp.float32)
    decay_rate = draw_decay_rate(jax.random.fold_in(key_list[8], 71), 0)
    return {"branch_x": branch_x, "positions": positions, "teacher_held": teacher_held, "gate_weights": gate_weights, "gate_bias": gate_bias, "conv_weight": conv_weight, "conv_bias": conv_bias, "decay_rate": decay_rate}


def one_sequence(inputs, gate_weights, gate_bias, conv_weight, conv_bias, decay_rate):
    rows, places, target = inputs
    rows_f = rows.astype(jnp.float32)
    padded = jnp.concatenate([jnp.zeros((3, R), jnp.float32), rows_f], axis=0)
    conv = jnp.zeros((LEN, R), jnp.float32) + conv_bias
    for lag_steps in range(4):
        valid = (places >= lag_steps).astype(jnp.float32)[:, None]
        conv = conv + conv_weight[lag_steps] * padded[3 - lag_steps:3 - lag_steps + LEN] * valid
    conv_rounded = conv.astype(jnp.bfloat16)
    conv_f = conv_rounded.astype(jnp.float32)
    weights_f = gate_weights.astype(jnp.float32)
    preact = jnp.einsum('thi,hgij->thgj', conv_f.reshape(LEN, HEADS, HS), weights_f)
    gate_x = jax.nn.sigmoid(preact[:, :, 0, :].reshape(LEN, R) + gate_bias[0])
    gate_a = jax.nn.sigmoid(preact[:, :, 1, :].reshape(LEN, R) + gate_bias[1])
    log_a = -8.0 * gate_a * decay_rate / LEN
    reset = (places == 0)[:, None]
    decay = jnp.where(reset, jnp.float32(0.0), jnp.exp(log_a))
    scale = jnp.where(reset, jnp.float32(1.0), jnp.sqrt(-jnp.expm1(2.0 * log_a)))
    drive = conv_f * gate_x * scale

    def advance(state, pair):
        state = pair[0] * state + pair[1]
        return (state, state)
    _, states = lax.scan(advance, jnp.zeros((R,), jnp.float32), (decay, drive))
    student = states.astype(jnp.bfloat16)
    student_f = student.astype(jnp.float32)
    normed = student_f * lax.rsqrt(lax.optimization_barrier(jnp.mean(student_f * student_f, axis=-1, keepdims=True)) + 1e-06)
    loss = lax.optimization_barrier(jnp.mean((normed - target.astype(jnp.float32)) ** 2, axis=-1))
    return (student, loss)

def reference(branch_x, positions, teacher_held, gate_weights, gate_bias, conv_weight, conv_bias, decay_rate):
    targets = jnp.roll(teacher_held, -(SEQS // 2), axis=0)

    def apply_one(inputs):
        return one_sequence(inputs, gate_weights, gate_bias, conv_weight, conv_bias, decay_rate)
    student_out, token_loss = lax.map(apply_one, (branch_x, positions, targets))
    return (student_out, token_loss)
```

```python
import functools

import jax
import jax.numpy as jnp
from jax import lax
from jax.experimental import pallas as pl
from jax.experimental.pallas import tpu as pltpu
from jax.sharding import PartitionSpec as P

HS = 128
MESH = pl.DeviceIdType.MESH
F32 = jnp.float32
BF16 = jnp.bfloat16
SIZES = (1, 2, 2, 2, 1)
BATCHES = len(SIZES)


def sigmoid(v):
    return 1.0 / (1.0 + jnp.exp(-v))


def minus_expm1(y, ey):
    series = 1.0 + y * (1 / 2 + y * (1 / 6 + y * (1 / 24 + y * (1 / 120 + y * (1 / 720)))))
    return jnp.where(y > -0.125, -y * series, 1.0 - ey)


def kernel(
    seq_len,
    x_hbm,
    pos_hbm,
    teach_hbm,
    gw_hbm,
    gb_hbm,
    cw_hbm,
    cb_hbm,
    rate_hbm,
    out_hbm,
    loss_ref,
    x_v,
    halo,
    pos_v,
    gb_v,
    cw_v,
    cb_v,
    rate_v,
    tbuf,
    wbuf,
    convb,
    prod_b,
    local_b,
    comp,
    rowc,
    tot,
    ysum,
    inc_b,
    xf,
    masks,
    tmp,
    acc_b,
    student,
    load_sem,
    out_sem,
    far_s,
    far_r,
    near_s,
    near_r,
    x_s,
    x_r,
    chip_s,
    chip_r,
    row_s,
    row_r,
    y_s,
    y_r,
    t_s,
    t_r,
    h_s,
    h_r,
):
    g, z, s = lax.axis_index("segment"), lax.axis_index("fsdp"), lax.axis_index("seq")
    planes, places = lax.axis_size("fsdp"), lax.axis_size("seq")
    row, here = s // 8, s % 8
    xc, core = here // 2, s % 2
    relay = lax.rem(z, 2) == core

    def at_z(dz):
        return (g, lax.rem(z + dz + planes, planes), s)

    def in_row(other):
        return (g, z, row * 8 + other)

    def remote(src, dst, send, recv, to):
        return pltpu.make_async_remote_copy(
            src_ref=src, dst_ref=dst, send_sem=send, recv_sem=recv, device_id=to, device_id_type=MESH
        )

    def await_bytes(ref, sem):
        pltpu.make_async_copy(ref, ref, sem).wait()

    loads = [
        pltpu.make_async_copy(gw_hbm.at[0], wbuf.at[0], load_sem.at[0]),
        pltpu.make_async_copy(x_hbm.at[0], x_v, load_sem.at[1]),
        pltpu.make_async_copy(pos_hbm, pos_v, load_sem.at[2]),
        pltpu.make_async_copy(cw_hbm, cw_v, load_sem.at[3]),
        pltpu.make_async_copy(cb_hbm, cb_v, load_sem.at[4]),
        pltpu.make_async_copy(gb_hbm, gb_v, load_sem.at[5]),
        pltpu.make_async_copy(rate_hbm, rate_v, load_sem.at[6]),
    ]
    for copy in loads:
        copy.start()

    partner = (1 - g, z, s)
    other_core = in_row(here // 2 * 2 + 1 - core)
    greeted = [at_z(4), at_z(-4), at_z(2), at_z(-2), at_z(1), at_z(-1), partner]
    greeted += [in_row(lax.rem(here + d, 8)) for d in range(1, 8)]
    greeted += [(g, z, lax.rem(s + 8, places))]
    greeted += [(g, z, lax.rem(s + 1, places)), (g, z, lax.rem(s + places - 1, places))]
    barrier = pltpu.get_barrier_semaphore()
    for device in greeted:
        pl.semaphore_signal(barrier, inc=1, device_id=device, device_id_type=MESH)
    loads[0].wait()
    pl.semaphore_wait(barrier, len(greeted))

    quarter = pl.ds(pl.multiple_of(xc * 32, 32), 32)

    def first(j, kind):
        return 8 * j + kind * SIZES[j]

    def piece(u, count):
        return wbuf.at[pl.ds(u, count), :, quarter, :]

    def far_copy(j, down):
        source = 8 * (j - 1) + (1 if down and j > 1 else 0)
        target = 8 * j + (1 if down else 0)
        k = j - 1 + (4 if down else 0)
        return remote(piece(source, 1), piece(target, 1), far_s.at[k], far_r.at[k], at_z(-4 if down else 4))

    def send_near(j):
        count = SIZES[j]
        src = piece(first(j, 0), count)
        for kind, dz in ((3, 2), (1, 1), (2, -1)):
            dst = piece(first(j, kind), count)
            remote(src, dst, near_s.at[j], near_r.at[kind, j], at_z(dz)).start()

    def wait_near(j, kind):
        dst = piece(first(j, kind), SIZES[j])
        await_bytes(dst, near_r.at[kind, j])

    def send_x(j, kind):
        src = piece(first(j, kind), SIZES[j])
        for d in (1, 3, 2):
            to = in_row(lax.rem(xc + d, 4) * 2 + core)
            remote(src, src, x_s.at[kind, j], x_r.at[kind, j], to).start()

    def three(j, kind):
        return wbuf.at[pl.ds(first(j, kind), SIZES[j]), :, pl.ds(0, 96), :]

    def chip_copy(j, kind):
        src = wbuf.at[pl.ds(first(j, kind), SIZES[j])]
        return remote(src, src, chip_s.at[kind, j], chip_r.at[kind, j], other_core)

    def both(for_relay, for_other):
        @pl.when(relay)
        def _():
            for_relay()

        @pl.when(jnp.logical_not(relay))
        def _():
            for_other()

    def start_far(j):
        far_copy(j, False).start()
        if j < 4:
            far_copy(j, True).start()

    def step_far(j):
        @pl.when(relay)
        def _():
            far_copy(j, False).wait_recv()
            if j < 4:
                far_copy(j, True).wait_recv()
                start_far(j + 1)
            send_near(j)
            send_x(j, 0)

    def step_near(j):
        def for_relay():
            wait_near(j, 3)
            send_x(j, 3)

        def for_other():
            for kind in (1, 2):
                wait_near(j, kind)
                send_x(j, kind)

        both(for_relay, for_other)

    def step_x(j):
        def for_relay():
            for kind in (0, 3) if j else (3,):
                await_bytes(three(j, kind), x_r.at[kind, j])
                chip_copy(j, kind).start()

        def for_other():
            for kind in (1, 2):
                await_bytes(three(j, kind), x_r.at[kind, j])
                chip_copy(j, kind).start()

        both(for_relay, for_other)

    def step_chip(j):
        def for_relay():
            for kind in (1, 2):
                chip_copy(j, kind).wait_recv()

        def for_other():
            for kind in (0, 3) if j else (3,):
                chip_copy(j, kind).wait_recv()

        both(for_relay, for_other)

    @pl.when(relay)
    def _():
        start_far(1)
        send_near(0)

    halo_copy = remote(x_hbm.at[0, pl.ds(112, 16), :], halo, h_s, h_r, (g, z, lax.rem(s + 1, places)))
    teacher_copy = remote(teach_hbm.at[0], tbuf, t_s, t_r, partner)

    @pl.when(s < places - 1)
    def _():
        halo_copy.start()

    teacher_copy.start()
    for copy in loads[1:]:
        copy.wait()

    pos = jnp.transpose(jnp.broadcast_to(pos_v[...].astype(F32), (HS, HS)))
    tmp[...] = pos
    for v in range(16):
        places_v = tmp[pl.ds(v, 8, stride=16), :]
        for k in range(3):
            masks[k, pl.ds(8 * v, 8), :] = (places_v >= k + 1.0).astype(F32)
    comp[...] = jnp.zeros_like(comp)
    acc_b[...] = jnp.zeros_like(acc_b)

    def columns(head):
        return pl.ds(pl.multiple_of(head * HS, HS), HS)

    @pl.when(s > 0)
    def _():
        halo_copy.wait_recv()

    @pl.when(s == 0)
    def _():
        halo[...] = jnp.zeros_like(halo)

    def conv_head(head, _):
        cols = columns(head)
        xf[pl.ds(0, 16), :] = halo[:, cols].astype(F32)
        xf[pl.ds(16, HS), :] = x_v[:, cols].astype(F32)
        rows = {v: xf[pl.ds(16 + v, 8, stride=16), :] for v in range(-3, 16)}
        taps = [cw_v[pl.ds(k, 1), cols] for k in range(4)]
        bias = cb_v[:, cols]
        out = []
        for v in range(16):
            total = bias + taps[0] * rows[v]
            for k in range(1, 4):
                total = total + taps[k] * rows[v - k] * masks[k - 1, pl.ds(8 * v, 8), :]
            out.append(total)
        convb[head] = jnp.concatenate(out, axis=0).astype(BF16)
        return 0

    def head_of(j, index):
        count = SIZES[j]
        kind, side = index // count, index % count
        ahead = jnp.where(kind == 0, 0, jnp.where(kind == 1, -1, jnp.where(kind == 2, 1, -2)))
        return lax.rem(z + ahead + jnp.where(side == 0, -4 * j, 4 * j) + 2 * planes, planes)

    sub = lax.broadcasted_iota(jnp.int32, (8, HS), 0)

    def gates(j, index, _):
        u = 8 * j + index
        head = head_of(j, index)
        cols = columns(head)
        rows_b = convb[head]
        pre_x = jnp.dot(rows_b, wbuf[u, 0], preferred_element_type=F32)
        pre_a = jnp.dot(rows_b, wbuf[u, 1], preferred_element_type=F32)
        gate_x = sigmoid(pre_x + gb_v[pl.ds(0, 1), cols])
        gate_a = sigmoid(pre_a + gb_v[pl.ds(1, 1), cols])
        log_a = gate_a * (rate_v[:, cols] * (-8.0 / seq_len))
        keep = masks[0]
        decay = jnp.exp(log_a)
        scale = jnp.sqrt(minus_expm1(2.0 * log_a, decay * decay))
        scale = jnp.where(keep > 0.0, scale, 1.0)
        decay = decay * keep
        drive = rows_b.astype(F32) * gate_x * scale
        prods, states = [decay[0:8]], [drive[0:8]]
        for v in range(1, 16):
            step = decay[8 * v : 8 * v + 8]
            prods.append(prods[-1] * step)
            states.append(step * states[-1] + drive[8 * v : 8 * v + 8])
        p, q = prods[-1], states[-1]
        for d in (1, 2, 4):
            inside = sub >= d
            p_before = jnp.where(inside, pltpu.roll(p, d, 0), 1.0)
            q_before = jnp.where(inside, pltpu.roll(q, d, 0), 0.0)
            q = p * q_before + q
            p = p * p_before
        p_in = jnp.where(sub >= 1, pltpu.roll(p, 1, 0), 1.0)
        q_in = jnp.where(sub >= 1, pltpu.roll(q, 1, 0), 0.0)
        comp[0, pl.ds(u, 1), :] = p[7:8]
        comp[1, pl.ds(u, 1), :] = q[7:8]
        for v in range(16):
            prod_b[u, pl.ds(8 * v, 8), :] = prods[v] * p_in
            local_b[u, pl.ds(8 * v, 8), :] = states[v] + prods[v] * q_in
        return 0

    def compute(j, begin, end):
        lax.fori_loop(begin, end, functools.partial(gates, j), 0)

    def mine(j):
        return pl.ds(8 * j, 8)

    def send_row(j):
        rowc[here, :, mine(j), :] = comp[:, mine(j), :]
        src = comp.at[:, mine(j), :]
        for d in range(1, 8):
            to = in_row(lax.rem(here + d, 8))
            remote(src, rowc.at[here, :, mine(j), :], row_s.at[j], row_r.at[j], to).start()

    def seven(j):
        return rowc.at[pl.ds(0, 7), :, mine(j), :]

    def y_copy(j):
        to = (g, z, lax.rem(s + 8, places))
        return remote(tot.at[mine(j)], ysum.at[mine(j)], y_s.at[j], y_r.at[j], to)

    def step_row(j):
        await_bytes(seven(j), row_r.at[j])
        all_p = jnp.zeros((8, HS), F32) + 1.0
        before_p, before_q, all_q = all_p, jnp.zeros((8, HS), F32), jnp.zeros((8, HS), F32)
        for k in range(8):
            a, b = rowc[k, 0, mine(j), :], rowc[k, 1, mine(j), :]
            before_p = jnp.where(k < here, before_p * a, before_p)
            before_q = jnp.where(k < here, a * before_q + b, before_q)
            all_q = a * all_q + b
        tot[mine(j), :] = all_q

        @pl.when(row == 0)
        def _():
            y_copy(j).start()

        inc_b[0, mine(j), :] = before_p
        inc_b[1, mine(j), :] = before_q

    def step_y(j):
        @pl.when(row == 1)
        def _():
            y_copy(j).wait_recv()
            inc_b[1, mine(j), :] = inc_b[0, mine(j), :] * ysum[mine(j), :] + inc_b[1, mine(j), :]

        def finish(index, _):
            u = 8 * j + index
            cols = columns(head_of(j, index))
            entering = inc_b[1, pl.ds(u, 1), :]
            for v in range(16):
                full = local_b[u, pl.ds(8 * v, 8), :] + prod_b[u, pl.ds(8 * v, 8), :] * entering
                tmp[pl.ds(v, 8, stride=16), :] = full
            rounded = tmp[...].astype(BF16)
            student[:, cols] = rounded
            wide = rounded.astype(F32)
            acc_b[...] += wide * wide
            return 0

        lax.fori_loop(0, 4 * SIZES[j], finish, 0)

    heads = x_v.shape[1] // HS
    lax.fori_loop(0, heads // 2, conv_head, 0)
    step_near(0)
    step_far(1)
    lax.fori_loop(heads // 2, heads, conv_head, 0)
    for j in range(BATCHES):
        step_x(j)
        if j + 1 < BATCHES:
            step_near(j + 1)
        if j + 2 < BATCHES:
            step_far(j + 2)
        step_chip(j)
        compute(j, 0, 2 * SIZES[j])
        if j:
            step_row(j - 1)
        compute(j, 2 * SIZES[j], 4 * SIZES[j])
        send_row(j)
        if j:
            step_y(j - 1)
    step_row(BATCHES - 1)
    step_y(BATCHES - 1)

    out_copy = pltpu.make_async_copy(student, out_hbm.at[0], out_sem)
    out_copy.start()
    width = x_v.shape[1]
    mean_sq = jnp.sum(acc_b[...], axis=1, keepdims=True) * (1.0 / width)
    tmp[...] = jnp.broadcast_to(lax.rsqrt(mean_sq + 1e-06), (HS, HS))
    acc_b[...] = jnp.zeros_like(acc_b)
    teacher_copy.wait_recv()

    def loss_head(head, _):
        cols = columns(head)
        diff = student[:, cols].astype(F32) * tmp[...] - tbuf[:, cols].astype(F32)
        acc_b[...] += diff * diff
        return 0

    lax.fori_loop(0, heads, loss_head, 0)
    loss_ref[...] = jnp.sum(jnp.transpose(acc_b[...]), axis=0, keepdims=True) * (1.0 / width)

    teacher_copy.wait_send()

    @pl.when(s < places - 1)
    def _():
        halo_copy.wait_send()

    @pl.when(row == 0)
    def _():
        for j in range(BATCHES):
            y_copy(j).wait_send()

    for j in range(BATCHES):
        await_bytes(seven(j), row_s.at[j])

    def sent_by_relay():
        for j in range(1, BATCHES):
            far_copy(j, False).wait_send()
            if j < 4:
                far_copy(j, True).wait_send()
        for j in range(BATCHES):
            await_bytes(three(j, 0), near_s.at[j])
            for kind in (0, 3) if j else (3,):
                await_bytes(three(j, kind), x_s.at[kind, j])
                chip_copy(j, kind).wait_send()

    def sent_by_other():
        for j in range(BATCHES):
            for kind in (1, 2):
                await_bytes(three(j, kind), x_s.at[kind, j])
                chip_copy(j, kind).wait_send()

    both(sent_by_relay, sent_by_other)
    out_copy.wait()


def local(branch_x, positions, teacher, gate_weights, gate_bias, conv_weight, conv_bias, decay_rate):
    rows, width = branch_x.shape[1:]
    seq_len = rows * lax.axis_size("seq")
    slots = 8 * BATCHES
    dma = pltpu.SemaphoreType.DMA
    out, loss = pl.pallas_call(
        functools.partial(kernel, seq_len),
        out_shape=(
            jax.ShapeDtypeStruct((1, rows, width), BF16),
            jax.ShapeDtypeStruct((1, rows), F32),
        ),
        in_specs=[pl.BlockSpec(memory_space=pltpu.HBM)] * 8,
        out_specs=(pl.BlockSpec(memory_space=pltpu.HBM), pl.BlockSpec(memory_space=pltpu.VMEM)),
        scratch_shapes=[
            pltpu.VMEM((rows, width), BF16),
            pltpu.VMEM((16, width), BF16),
            pltpu.VMEM((1, rows), jnp.int32),
            pltpu.VMEM((2, width), F32),
            pltpu.VMEM((4, width), F32),
            pltpu.VMEM((1, width), F32),
            pltpu.VMEM((1, width), F32),
            pltpu.VMEM((rows, width), BF16),
            pltpu.VMEM((slots, 2, HS, HS), BF16),
            pltpu.VMEM((width // HS, rows, HS), BF16),
            pltpu.VMEM((slots, rows, HS), F32),
            pltpu.VMEM((slots, rows, HS), F32),
            pltpu.VMEM((2, slots, HS), F32),
            pltpu.VMEM((8, 2, slots, HS), F32),
            pltpu.VMEM((slots, HS), F32),
            pltpu.VMEM((slots, HS), F32),
            pltpu.VMEM((2, slots, HS), F32),
            pltpu.VMEM((rows + 16, HS), F32),
            pltpu.VMEM((3, rows, HS), F32),
            pltpu.VMEM((rows, HS), F32),
            pltpu.VMEM((rows, HS), F32),
            pltpu.VMEM((rows, width), BF16),
            dma((7,)),
            dma,
            dma((8,)),
            dma((8,)),
            dma((BATCHES,)),
            dma((4, BATCHES)),
            dma((4, BATCHES)),
            dma((4, BATCHES)),
            dma((4, BATCHES)),
            dma((4, BATCHES)),
            dma((BATCHES,)),
            dma((BATCHES,)),
            dma((BATCHES,)),
            dma((BATCHES,)),
            dma,
            dma,
            dma,
            dma,
        ],
        compiler_params=pltpu.CompilerParams(
            collective_id=0, has_side_effects=True, vmem_limit_bytes=60 << 20
        ),
        name="step",
    )(
        branch_x,
        positions,
        teacher,
        gate_weights,
        gate_bias,
        conv_weight,
        conv_bias.reshape(1, width),
        decay_rate.reshape(1, width),
    )
    return out, loss


def solution(mesh):
    in_specs = (
        P(("segment", "fsdp"), "seq", None),
        P(("segment", "fsdp"), "seq"),
        P(("segment", "fsdp"), "seq", None),
        P("fsdp", None, None, None),
        P(),
        P(),
        P(),
        P(),
    )
    out_specs = (P(("segment", "fsdp"), "seq", None), P(("segment", "fsdp"), "seq"))
    return jax.shard_map(local, mesh=mesh, in_specs=in_specs, out_specs=out_specs, check_vma=False)
```

```python
import functools

import jax
import jax.numpy as jnp
from jax import lax
from jax.experimental import pallas as pl
from jax.experimental.pallas import tpu as pltpu
from jax.sharding import PartitionSpec as P

HS = 128
MESH = pl.DeviceIdType.MESH
F32 = jnp.float32
BF16 = jnp.bfloat16
SIZES = (1, 2, 2, 2, 1)
BATCHES = len(SIZES)
LAST = BATCHES - 1


def sigmoid(v):
    return 1.0 / (1.0 + jnp.exp(-v))


def minus_expm1(y, ey):
    series = 1.0 + y * (1 / 2 + y * (1 / 6 + y * (1 / 24 + y * (1 / 120 + y * (1 / 720)))))
    return jnp.where(y > -0.125, -y * series, 1.0 - ey)


def kernel(
    seq_len,
    x_hbm,
    pos_hbm,
    teach_hbm,
    gw_hbm,
    gb_hbm,
    cw_hbm,
    cb_hbm,
    rate_hbm,
    out_hbm,
    loss_ref,
    x_v,
    halo,
    pos_v,
    gb_v,
    cw_v,
    cb_v,
    rate_v,
    tbuf,
    wbuf,
    convb,
    prod_b,
    local_b,
    comp,
    rowc,
    allc,
    tot,
    ysum,
    inc_b,
    xf,
    masks,
    tmp,
    acc_b,
    student,
    load_sem,
    out_sem,
    far_s,
    far_r,
    near_s,
    near_r,
    x_s,
    x_r,
    chip_s,
    chip_r,
    row_s,
    row_r,
    all_s,
    all_r,
    y_s,
    y_r,
    t_s,
    t_r,
    h_s,
    h_r,
):
    g, z, s = lax.axis_index("segment"), lax.axis_index("fsdp"), lax.axis_index("seq")
    planes, places = lax.axis_size("fsdp"), lax.axis_size("seq")
    row, here = s // 8, s % 8
    xc, core = here // 2, s % 2
    relay = lax.rem(z, 2) == core

    def at_z(dz):
        return (g, lax.rem(z + dz + planes, planes), s)

    def in_row(other):
        return (g, z, row * 8 + other)

    def remote(src, dst, send, recv, to):
        return pltpu.make_async_remote_copy(
            src_ref=src, dst_ref=dst, send_sem=send, recv_sem=recv, device_id=to, device_id_type=MESH
        )

    def await_bytes(ref, sem):
        pltpu.make_async_copy(ref, ref, sem).wait()

    loads = [
        pltpu.make_async_copy(gw_hbm.at[0], wbuf.at[0], load_sem.at[0]),
        pltpu.make_async_copy(x_hbm.at[0], x_v, load_sem.at[1]),
        pltpu.make_async_copy(pos_hbm, pos_v, load_sem.at[2]),
        pltpu.make_async_copy(cw_hbm, cw_v, load_sem.at[3]),
        pltpu.make_async_copy(cb_hbm, cb_v, load_sem.at[4]),
        pltpu.make_async_copy(gb_hbm, gb_v, load_sem.at[5]),
        pltpu.make_async_copy(rate_hbm, rate_v, load_sem.at[6]),
    ]
    for copy in loads:
        copy.start()

    partner = (1 - g, z, s)
    other_core = in_row(here // 2 * 2 + 1 - core)
    greeted = [at_z(dz) for dz in (8, -8, 4, -4)]
    for dz in (2, -2, 1, -1):
        for d in range(4):
            greeted.append(at_z(dz)[:2] + (row * 8 + lax.rem(xc + d, 4) * 2 + core,))
    greeted += [partner] + [(g, z, lax.rem(s + d, places)) for d in range(1, 16)]
    barrier = pltpu.get_barrier_semaphore()
    for device in greeted:
        pl.semaphore_signal(barrier, inc=1, device_id=device, device_id_type=MESH)
    loads[0].wait()
    pl.semaphore_wait(barrier, len(greeted))

    blocks = [pl.ds(32 * k, 32) for k in range(4)]
    quarter = pl.ds(pl.multiple_of(xc * 32, 32), 32)

    def first(j, kind):
        return 8 * j + kind * SIZES[j]

    def piece(u, count):
        return wbuf.at[pl.ds(u, count), :, quarter, :]

    def far_copy(j, down):
        source = (8 * 2 + (1 if down else 0)) if j > 2 else 0
        target = 8 * j + (1 if down else 0)
        k = j - 1 + (4 if down else 0)
        dz = 4 if j % 2 else 8
        return remote(piece(source, 1), piece(target, 1), far_s.at[k], far_r.at[k], at_z(-dz if down else dz))

    def send_near(j):
        count = SIZES[j]
        src = piece(first(j, 0), count)
        for d in (2, 1, 3, 0) if j == LAST else (0,):
            place = row * 8 + lax.rem(xc + d, 4) * 2 + core
            for kind, dz in ((3, 2), (1, 1), (2, -1)):
                dst = piece(first(j, kind), count)
                to = (g, lax.rem(z + dz + planes, planes), place)
                remote(src, dst, near_s.at[j], near_r.at[kind, j], to).start()

    def wait_near(j, kind):
        dst = piece(first(j, kind), SIZES[j])
        await_bytes(dst, near_r.at[kind, j])

    def send_x(j, kind):
        src = piece(first(j, kind), SIZES[j])
        for d in (1, 3, 2):
            to = in_row(lax.rem(xc + d, 4) * 2 + core)
            remote(src, src, x_s.at[kind, j], x_r.at[kind, j], to).start()

    def three(j, kind):
        return wbuf.at[pl.ds(first(j, kind), SIZES[j]), :, pl.ds(0, 96), :]

    def await_x(j, kind):
        if j == LAST and kind:
            await_bytes(wbuf.at[pl.ds(first(j, kind), 1)], near_r.at[kind, j])
        else:
            await_bytes(three(j, kind), x_r.at[kind, j])

    def chip_copy(j, kind):
        src = wbuf.at[pl.ds(first(j, kind), SIZES[j])]
        return remote(src, src, chip_s.at[kind, j], chip_r.at[kind, j], other_core)

    def both(for_relay, for_other):
        @pl.when(relay)
        def _():
            for_relay()

        @pl.when(jnp.logical_not(relay))
        def _():
            for_other()

    def start_far(j):
        far_copy(j, False).start()
        if j < 4:
            far_copy(j, True).start()

    def step_far(j):
        @pl.when(relay)
        def _():
            far_copy(j, False).wait_recv()
            if j < 4:
                far_copy(j, True).wait_recv()
            if j == 2:
                start_far(4)
                start_far(3)
            send_near(j)
            send_x(j, 0)

    def step_near(j):
        if j == LAST:
            return

        def for_relay():
            wait_near(j, 3)
            send_x(j, 3)

        def for_other():
            for kind in (1, 2):
                wait_near(j, kind)
                send_x(j, kind)

        both(for_relay, for_other)

    def step_x(j):
        def for_relay():
            for kind in (0, 3) if j else (3,):
                await_x(j, kind)
                chip_copy(j, kind).start()

        def for_other():
            for kind in (1, 2):
                await_x(j, kind)
                chip_copy(j, kind).start()

        both(for_relay, for_other)

    def step_chip(j):
        def for_relay():
            for kind in (1, 2):
                chip_copy(j, kind).wait_recv()

        def for_other():
            for kind in (0, 3) if j else (3,):
                chip_copy(j, kind).wait_recv()

        both(for_relay, for_other)

    @pl.when(relay)
    def _():
        start_far(2)
        start_far(1)
        send_near(0)

    halo_copy = remote(x_hbm.at[0, pl.ds(112, 16), :], halo, h_s, h_r, (g, z, lax.rem(s + 1, places)))
    teacher_copies = [
        remote(teach_hbm.at[0, block, :], tbuf.at[block, :], t_s.at[k], t_r.at[k], partner)
        for k, block in enumerate(blocks)
    ]

    @pl.when(s < places - 1)
    def _():
        halo_copy.start()

    for copy in teacher_copies:
        copy.start()
    for copy in loads[1:]:
        copy.wait()

    pos = jnp.transpose(jnp.broadcast_to(pos_v[...].astype(F32), (HS, HS)))
    tmp[...] = pos
    for v in range(16):
        places_v = tmp[pl.ds(v, 8, stride=16), :]
        for k in range(3):
            masks[k, pl.ds(8 * v, 8), :] = (places_v >= k + 1.0).astype(F32)
    comp[...] = jnp.zeros_like(comp)
    acc_b[...] = jnp.zeros_like(acc_b)

    def columns(head):
        return pl.ds(pl.multiple_of(head * HS, HS), HS)

    @pl.when(s > 0)
    def _():
        halo_copy.wait_recv()

    @pl.when(s == 0)
    def _():
        halo[...] = jnp.zeros_like(halo)

    def conv_head(head, _):
        cols = columns(head)
        xf[pl.ds(0, 16), :] = halo[:, cols].astype(F32)
        xf[pl.ds(16, HS), :] = x_v[:, cols].astype(F32)
        rows = {v: xf[pl.ds(16 + v, 8, stride=16), :] for v in range(-3, 16)}
        taps = [cw_v[pl.ds(k, 1), cols] for k in range(4)]
        bias = cb_v[:, cols]
        out = []
        for v in range(16):
            total = bias + taps[0] * rows[v]
            for k in range(1, 4):
                total = total + taps[k] * rows[v - k] * masks[k - 1, pl.ds(8 * v, 8), :]
            out.append(total)
        convb[head] = jnp.concatenate(out, axis=0).astype(BF16)
        return 0

    def head_of(j, index):
        count = SIZES[j]
        kind, side = index // count, index % count
        ahead = jnp.where(kind == 0, 0, jnp.where(kind == 1, -1, jnp.where(kind == 2, 1, -2)))
        return lax.rem(z + ahead + jnp.where(side == 0, -4 * j, 4 * j) + 2 * planes, planes)

    sub = lax.broadcasted_iota(jnp.int32, (8, HS), 0)

    def gates(j, index, _):
        u = 8 * j + index
        head = head_of(j, index)
        cols = columns(head)
        rows_b = convb[head]
        pre_x = jnp.dot(rows_b, wbuf[u, 0], preferred_element_type=F32)
        pre_a = jnp.dot(rows_b, wbuf[u, 1], preferred_element_type=F32)
        gate_x = sigmoid(pre_x + gb_v[pl.ds(0, 1), cols])
        gate_a = sigmoid(pre_a + gb_v[pl.ds(1, 1), cols])
        log_a = gate_a * (rate_v[:, cols] * (-8.0 / seq_len))
        keep = masks[0]
        decay = jnp.exp(log_a)
        scale = jnp.sqrt(minus_expm1(2.0 * log_a, decay * decay))
        scale = jnp.where(keep > 0.0, scale, 1.0)
        decay = decay * keep
        drive = rows_b.astype(F32) * gate_x * scale
        prods, states = [decay[0:8]], [drive[0:8]]
        for v in range(1, 16):
            step = decay[8 * v : 8 * v + 8]
            prods.append(prods[-1] * step)
            states.append(step * states[-1] + drive[8 * v : 8 * v + 8])
        p, q = prods[-1], states[-1]
        for d in (1, 2, 4):
            inside = sub >= d
            p_before = jnp.where(inside, pltpu.roll(p, d, 0), 1.0)
            q_before = jnp.where(inside, pltpu.roll(q, d, 0), 0.0)
            q = p * q_before + q
            p = p * p_before
        p_in = jnp.where(sub >= 1, pltpu.roll(p, 1, 0), 1.0)
        q_in = jnp.where(sub >= 1, pltpu.roll(q, 1, 0), 0.0)
        comp[0, pl.ds(u, 1), :] = p[7:8]
        comp[1, pl.ds(u, 1), :] = q[7:8]
        for v in range(16):
            prod_b[u, pl.ds(8 * v, 8), :] = prods[v] * p_in
            local_b[u, pl.ds(8 * v, 8), :] = states[v] + prods[v] * q_in
        return 0

    def compute(j, begin, end):
        lax.fori_loop(begin, end, functools.partial(gates, j), 0, unroll=4)

    def mine(j):
        return pl.ds(8 * j, 8)

    def send_row(j):
        rowc[here, :, mine(j), :] = comp[:, mine(j), :]
        src = comp.at[:, mine(j), :]
        for d in range(1, 8):
            to = in_row(lax.rem(here + d, 8))
            remote(src, rowc.at[here, :, mine(j), :], row_s.at[j], row_r.at[j], to).start()

    def last_copy(d):
        mine_last = pl.ds(8 * LAST, 8)
        to = (g, z, lax.rem(s + d, places))
        return remote(comp.at[:, mine_last, :], allc.at[s], all_s.at[d - 1], all_r.at[s], to)

    def send_last():
        for d in range(15, 0, -1):

            @pl.when(s + d < places)
            def _():
                last_copy(d).start()

    def step_last():
        entering = jnp.zeros((8, HS), F32)
        for k in range(15):

            @pl.when(k < s)
            def _():
                pltpu.make_async_copy(allc.at[k], allc.at[k], all_r.at[k]).wait()

        for k in range(15):
            through = allc[k, 0] * entering + allc[k, 1]
            entering = jnp.where(k < s, through, entering)
        inc_b[1, mine(LAST), :] = entering

    def seven(j):
        return rowc.at[pl.ds(0, 7), :, mine(j), :]

    def y_copy(j):
        to = (g, z, lax.rem(s + 8, places))
        return remote(tot.at[mine(j)], ysum.at[mine(j)], y_s.at[j], y_r.at[j], to)

    def step_row(j):
        await_bytes(seven(j), row_r.at[j])
        all_p = jnp.zeros((8, HS), F32) + 1.0
        before_p, before_q, all_q = all_p, jnp.zeros((8, HS), F32), jnp.zeros((8, HS), F32)
        for k in range(8):
            a, b = rowc[k, 0, mine(j), :], rowc[k, 1, mine(j), :]
            before_p = jnp.where(k < here, before_p * a, before_p)
            before_q = jnp.where(k < here, a * before_q + b, before_q)
            all_q = a * all_q + b
        tot[mine(j), :] = all_q

        @pl.when(row == 0)
        def _():
            y_copy(j).start()

        inc_b[0, mine(j), :] = before_p
        inc_b[1, mine(j), :] = before_q

    def step_y(j):
        @pl.when(row == 1)
        def _():
            y_copy(j).wait_recv()
            inc_b[1, mine(j), :] = inc_b[0, mine(j), :] * ysum[mine(j), :] + inc_b[1, mine(j), :]

        finish_batch(j)

    def finish_batch(j):
        def finish(index, _):
            u = 8 * j + index
            cols = columns(head_of(j, index))
            entering = inc_b[1, pl.ds(u, 1), :]
            for v in range(16):
                full = local_b[u, pl.ds(8 * v, 8), :] + prod_b[u, pl.ds(8 * v, 8), :] * entering
                tmp[pl.ds(v, 8, stride=16), :] = full
            rounded = tmp[...].astype(BF16)
            student[:, cols] = rounded
            wide = rounded.astype(F32)
            acc_b[...] += wide * wide
            return 0

        lax.fori_loop(0, 4 * SIZES[j], finish, 0, unroll=4)

    def sent(j):
        def by_relay():
            if j:
                far_copy(j, False).wait_send()
                if j < 4:
                    far_copy(j, True).wait_send()
            await_bytes(wbuf.at[pl.ds(0, 3)] if j == LAST else three(j, 0), near_s.at[j])
            for kind in (0, 3) if j else (3,):
                if j < LAST or kind == 0:
                    await_bytes(three(j, kind), x_s.at[kind, j])
                chip_copy(j, kind).wait_send()

        def by_other():
            for kind in (1, 2):
                if j < LAST:
                    await_bytes(three(j, kind), x_s.at[kind, j])
                chip_copy(j, kind).wait_send()

        both(by_relay, by_other)

    heads = x_v.shape[1] // HS
    lax.fori_loop(0, heads // 2, conv_head, 0, unroll=4)
    step_near(0)
    step_far(1)
    lax.fori_loop(heads // 2, heads, conv_head, 0, unroll=4)
    step_x(0)
    step_far(2)
    step_near(1)
    step_chip(0)
    compute(0, 0, 4)
    send_row(0)
    step_near(2)
    step_x(1)
    step_far(3)
    step_chip(1)
    compute(1, 0, 4)
    step_x(2)
    step_far(4)
    step_near(3)
    compute(1, 4, 8)
    send_row(1)
    step_row(0)
    step_chip(2)
    compute(2, 0, 4)
    step_x(3)
    step_x(4)
    step_y(0)
    compute(2, 4, 8)
    send_row(2)
    step_row(1)
    step_chip(3)
    compute(3, 0, 4)
    step_y(1)
    step_row(2)
    compute(3, 4, 8)
    send_row(3)
    step_chip(4)
    compute(4, 0, 4)
    send_last()
    step_y(2)
    step_row(3)
    for j in range(BATCHES):
        sent(j)
    step_y(3)
    step_last()
    finish_batch(LAST)

    out_copy = pltpu.make_async_copy(student, out_hbm.at[0], out_sem)
    out_copy.start()
    width = x_v.shape[1]
    mean_sq = jnp.sum(acc_b[...], axis=1, keepdims=True) * (1.0 / width)
    tmp[...] = jnp.broadcast_to(lax.rsqrt(mean_sq + 1e-06), (HS, HS))
    for k, block in enumerate(blocks):
        teacher_copies[k].wait_recv()

        def loss_head(head, total):
            cols = columns(head)
            diff = student[block, cols].astype(F32) * tmp[block, :] - tbuf[block, cols].astype(F32)
            return total + diff * diff

        acc_b[block, :] = lax.fori_loop(0, heads, loss_head, jnp.zeros((32, HS), F32), unroll=4)
    loss_ref[...] = jnp.sum(jnp.transpose(acc_b[...]), axis=0, keepdims=True) * (1.0 / width)

    for copy in teacher_copies:
        copy.wait_send()

    @pl.when(s < places - 1)
    def _():
        halo_copy.wait_send()

    @pl.when(row == 0)
    def _():
        for j in range(LAST):
            y_copy(j).wait_send()

    for j in range(LAST):
        await_bytes(seven(j), row_s.at[j])
    for d in range(1, 16):

        @pl.when(s + d < places)
        def _():
            last_copy(d).wait_send()

    out_copy.wait()


def local(branch_x, positions, teacher, gate_weights, gate_bias, conv_weight, conv_bias, decay_rate):
    rows, width = branch_x.shape[1:]
    seq_len = rows * lax.axis_size("seq")
    slots = 8 * BATCHES
    dma = pltpu.SemaphoreType.DMA
    operands = (
        branch_x,
        positions,
        teacher,
        gate_weights,
        gate_bias,
        conv_weight,
        conv_bias.reshape(1, width),
        decay_rate.reshape(1, width),
    )
    operands = [pltpu.with_memory_space_constraint(v, pltpu.HBM) for v in operands]
    out, loss = pl.pallas_call(
        functools.partial(kernel, seq_len),
        out_shape=(
            jax.ShapeDtypeStruct((1, rows, width), BF16),
            jax.ShapeDtypeStruct((1, rows), F32),
        ),
        in_specs=[pl.BlockSpec(memory_space=pltpu.HBM)] * 8,
        out_specs=(pl.BlockSpec(memory_space=pltpu.HBM), pl.BlockSpec(memory_space=pltpu.VMEM)),
        scratch_shapes=[
            pltpu.VMEM((rows, width), BF16),
            pltpu.VMEM((16, width), BF16),
            pltpu.VMEM((1, rows), jnp.int32),
            pltpu.VMEM((2, width), F32),
            pltpu.VMEM((4, width), F32),
            pltpu.VMEM((1, width), F32),
            pltpu.VMEM((1, width), F32),
            pltpu.VMEM((rows, width), BF16),
            pltpu.VMEM((slots, 2, HS, HS), BF16),
            pltpu.VMEM((width // HS, rows, HS), BF16),
            pltpu.VMEM((slots, rows, HS), F32),
            pltpu.VMEM((slots, rows, HS), F32),
            pltpu.VMEM((2, slots, HS), F32),
            pltpu.VMEM((8, 2, slots, HS), F32),
            pltpu.VMEM((16, 2, 8, HS), F32),
            pltpu.VMEM((slots, HS), F32),
            pltpu.VMEM((slots, HS), F32),
            pltpu.VMEM((2, slots, HS), F32),
            pltpu.VMEM((rows + 16, HS), F32),
            pltpu.VMEM((3, rows, HS), F32),
            pltpu.VMEM((rows, HS), F32),
            pltpu.VMEM((rows, HS), F32),
            pltpu.VMEM((rows, width), BF16),
            dma((7,)),
            dma,
            dma((8,)),
            dma((8,)),
            dma((BATCHES,)),
            dma((4, BATCHES)),
            dma((4, BATCHES)),
            dma((4, BATCHES)),
            dma((4, BATCHES)),
            dma((4, BATCHES)),
            dma((BATCHES,)),
            dma((BATCHES,)),
            dma((15,)),
            dma((16,)),
            dma((BATCHES,)),
            dma((BATCHES,)),
            dma((4,)),
            dma((4,)),
            dma,
            dma,
        ],
        compiler_params=pltpu.CompilerParams(
            collective_id=0, has_side_effects=True, vmem_limit_bytes=40 << 20
        ),
        name="step",
    )(*operands)
    return out, loss


def solution(mesh):
    in_specs = (
        P(("segment", "fsdp"), "seq", None),
        P(("segment", "fsdp"), "seq"),
        P(("segment", "fsdp"), "seq", None),
        P("fsdp", None, None, None),
        P(),
        P(),
        P(),
        P(),
    )
    out_specs = (P(("segment", "fsdp"), "seq", None), P(("segment", "fsdp"), "seq"))
    return jax.shard_map(local, mesh=mesh, in_specs=in_specs, out_specs=out_specs, check_vma=False)
```

```python
import functools

import jax
import jax.numpy as jnp
from jax import lax
from jax.experimental import pallas as pl
from jax.experimental.pallas import tpu as pltpu
from jax.sharding import PartitionSpec as P

HS = 128
MESH = pl.DeviceIdType.MESH
F32 = jnp.float32
BF16 = jnp.bfloat16
SIZES = (1, 2, 2, 2, 1)
BATCHES = len(SIZES)
LAST = BATCHES - 1
DIRECT = 3


def sigmoid(v):
    return 1.0 / (1.0 + jnp.exp(-v))


def minus_expm1(y, ey):
    series = 1.0 + y * (1 / 2 + y * (1 / 6 + y * (1 / 24 + y * (1 / 120 + y * (1 / 720)))))
    return jnp.where(y > -0.125, -y * series, 1.0 - ey)


def kernel(
    seq_len,
    x_hbm,
    pos_hbm,
    teach_hbm,
    gw_hbm,
    gb_hbm,
    cw_hbm,
    cb_hbm,
    rate_hbm,
    out_hbm,
    loss_ref,
    x_v,
    halo,
    pos_v,
    gb_v,
    cw_v,
    cb_v,
    rate_v,
    tbuf,
    wbuf,
    convb,
    prod_b,
    local_b,
    comp,
    rowc,
    allc,
    tot,
    ysum,
    inc_b,
    xf,
    masks,
    tmp,
    acc_b,
    student,
    load_sem,
    out_sem,
    far_s,
    far_r,
    near_s,
    near_r,
    x_s,
    x_r,
    chip_s,
    chip_r,
    row_s,
    row_r,
    all_s,
    all_r,
    y_s,
    y_r,
    t_s,
    t_r,
    h_s,
    h_r,
):
    g, z, s = lax.axis_index("segment"), lax.axis_index("fsdp"), lax.axis_index("seq")
    planes, places = lax.axis_size("fsdp"), lax.axis_size("seq")
    row, here = s // 8, s % 8
    xc, core = here // 2, s % 2
    relay = lax.rem(z, 2) == core

    def at_z(dz):
        return (g, lax.rem(z + dz + planes, planes), s)

    def in_row(other):
        return (g, z, row * 8 + other)

    def remote(src, dst, send, recv, to):
        return pltpu.make_async_remote_copy(
            src_ref=src, dst_ref=dst, send_sem=send, recv_sem=recv, device_id=to, device_id_type=MESH
        )

    def await_bytes(ref, sem):
        pltpu.make_async_copy(ref, ref, sem).wait()

    loads = [
        pltpu.make_async_copy(gw_hbm.at[0], wbuf.at[0], load_sem.at[0]),
        pltpu.make_async_copy(x_hbm.at[0], x_v, load_sem.at[1]),
        pltpu.make_async_copy(pos_hbm, pos_v, load_sem.at[2]),
        pltpu.make_async_copy(cw_hbm, cw_v, load_sem.at[3]),
        pltpu.make_async_copy(cb_hbm, cb_v, load_sem.at[4]),
        pltpu.make_async_copy(gb_hbm, gb_v, load_sem.at[5]),
        pltpu.make_async_copy(rate_hbm, rate_v, load_sem.at[6]),
    ]
    for copy in loads:
        copy.start()

    partner = (1 - g, z, s)
    other_core = in_row(here // 2 * 2 + 1 - core)
    greeted = [at_z(dz) for dz in (8, -8, 4, -4)]
    for dz in (2, -2, 1, -1):
        for d in range(4):
            greeted.append(at_z(dz)[:2] + (row * 8 + lax.rem(xc + d, 4) * 2 + core,))
    greeted += [partner] + [(g, z, lax.rem(s + d, places)) for d in range(1, 16)]
    barrier = pltpu.get_barrier_semaphore()
    for device in greeted:
        pl.semaphore_signal(barrier, inc=1, device_id=device, device_id_type=MESH)
    loads[0].wait()
    pl.semaphore_wait(barrier, len(greeted))

    blocks = [pl.ds(32 * k, 32) for k in range(4)]
    quarter = pl.ds(pl.multiple_of(xc * 32, 32), 32)

    def first(j, kind):
        return 8 * j + kind * SIZES[j]

    def piece(u, count):
        return wbuf.at[pl.ds(u, count), :, quarter, :]

    def far_copy(j, down):
        source = (8 * 2 + (1 if down else 0)) if j > 2 else 0
        target = 8 * j + (1 if down and j < 4 else 0)
        k = j - 1 + (4 if down else 0)
        dz = 4 if j % 2 else 8
        return remote(piece(source, 1), piece(target, 1), far_s.at[k], far_r.at[k], at_z(-dz if down else dz))

    def send_near(j):
        count = SIZES[j]
        src = piece(first(j, 0), count)
        for d in (2, 1, 3, 0) if j == LAST else (0,):
            place = row * 8 + lax.rem(xc + d, 4) * 2 + core
            for kind, dz in ((3, 2), (1, 1), (2, -1)):
                dst = piece(first(j, kind), count)
                to = (g, lax.rem(z + dz + planes, planes), place)
                remote(src, dst, near_s.at[j], near_r.at[kind, j], to).start()

    def wait_near(j, kind):
        dst = piece(first(j, kind), SIZES[j])
        await_bytes(dst, near_r.at[kind, j])

    def send_x(j, kind):
        src = piece(first(j, kind), SIZES[j])
        for d in (1, 3, 2):
            to = in_row(lax.rem(xc + d, 4) * 2 + core)
            remote(src, src, x_s.at[kind, j], x_r.at[kind, j], to).start()

    def three(j, kind):
        return wbuf.at[pl.ds(first(j, kind), SIZES[j]), :, pl.ds(0, 96), :]

    def await_x(j, kind):
        if j == LAST and kind:
            await_bytes(wbuf.at[pl.ds(first(j, kind), 1)], near_r.at[kind, j])
        else:
            await_bytes(three(j, kind), x_r.at[kind, j])

    def chip_copy(j, kind):
        src = wbuf.at[pl.ds(first(j, kind), SIZES[j])]
        return remote(src, src, chip_s.at[kind, j], chip_r.at[kind, j], other_core)

    def both(for_relay, for_other):
        @pl.when(relay)
        def _():
            for_relay()

        @pl.when(jnp.logical_not(relay))
        def _():
            for_other()

    def far_copies(j):
        return [far_copy(j, down) for down in ((False, True) if j < 4 else (True,))]

    def start_far(j):
        for copy in far_copies(j):
            copy.start()

    def step_far(j):
        @pl.when(relay)
        def _():
            for copy in far_copies(j):
                copy.wait_recv()
            if j == 2:
                start_far(4)
                start_far(3)
            send_near(j)
            send_x(j, 0)

    def step_near(j):
        if j == LAST:
            return

        def for_relay():
            wait_near(j, 3)
            send_x(j, 3)

        def for_other():
            for kind in (1, 2):
                wait_near(j, kind)
                send_x(j, kind)

        both(for_relay, for_other)

    def step_x(j):
        def for_relay():
            for kind in (0, 3) if j else (3,):
                await_x(j, kind)
                chip_copy(j, kind).start()

        def for_other():
            for kind in (1, 2):
                await_x(j, kind)
                chip_copy(j, kind).start()

        both(for_relay, for_other)

    def step_chip(j):
        def for_relay():
            for kind in (1, 2):
                chip_copy(j, kind).wait_recv()

        def for_other():
            for kind in (0, 3) if j else (3,):
                chip_copy(j, kind).wait_recv()

        both(for_relay, for_other)

    @pl.when(relay)
    def _():
        start_far(2)
        start_far(1)
        send_near(0)

    halo_copy = remote(x_hbm.at[0, pl.ds(112, 16), :], halo, h_s, h_r, (g, z, lax.rem(s + 1, places)))
    teacher_copies = [
        remote(teach_hbm.at[0, block, :], tbuf.at[block, :], t_s.at[k], t_r.at[k], partner)
        for k, block in enumerate(blocks)
    ]

    @pl.when(s < places - 1)
    def _():
        halo_copy.start()

    for copy in teacher_copies:
        copy.start()
    for copy in loads[1:]:
        copy.wait()

    pos = jnp.transpose(jnp.broadcast_to(pos_v[...].astype(F32), (HS, HS)))
    tmp[...] = pos
    for v in range(16):
        places_v = tmp[pl.ds(v, 8, stride=16), :]
        for k in range(3):
            masks[k, pl.ds(8 * v, 8), :] = (places_v >= k + 1.0).astype(F32)
    comp[...] = jnp.zeros_like(comp)
    acc_b[...] = jnp.zeros_like(acc_b)

    def columns(head):
        return pl.ds(pl.multiple_of(head * HS, HS), HS)

    @pl.when(s > 0)
    def _():
        halo_copy.wait_recv()

    @pl.when(s == 0)
    def _():
        halo[...] = jnp.zeros_like(halo)

    def conv_head(head, _):
        cols = columns(head)
        xf[pl.ds(0, 16), :] = halo[:, cols].astype(F32)
        xf[pl.ds(16, HS), :] = x_v[:, cols].astype(F32)
        rows = {v: xf[pl.ds(16 + v, 8, stride=16), :] for v in range(-3, 16)}
        taps = [cw_v[pl.ds(k, 1), cols] for k in range(4)]
        bias = cb_v[:, cols]
        out = []
        for v in range(16):
            total = bias + taps[0] * rows[v]
            for k in range(1, 4):
                total = total + taps[k] * rows[v - k] * masks[k - 1, pl.ds(8 * v, 8), :]
            out.append(total)
        convb[head] = jnp.concatenate(out, axis=0).astype(BF16)
        return 0

    def head_of(j, index):
        count = SIZES[j]
        kind, side = index // count, index % count
        ahead = jnp.where(kind == 0, 0, jnp.where(kind == 1, -1, jnp.where(kind == 2, 1, -2)))
        return lax.rem(z + ahead + jnp.where(side == 0, -4 * j, 4 * j) + 2 * planes, planes)

    sub = lax.broadcasted_iota(jnp.int32, (8, HS), 0)

    def gates(j, index, _):
        u = 8 * j + index
        head = head_of(j, index)
        cols = columns(head)
        rows_b = convb[head]
        pre_x = jnp.dot(rows_b, wbuf[u, 0], preferred_element_type=F32)
        pre_a = jnp.dot(rows_b, wbuf[u, 1], preferred_element_type=F32)
        gate_x = sigmoid(pre_x + gb_v[pl.ds(0, 1), cols])
        gate_a = sigmoid(pre_a + gb_v[pl.ds(1, 1), cols])
        log_a = gate_a * (rate_v[:, cols] * (-8.0 / seq_len))
        keep = masks[0]
        decay = jnp.exp(log_a)
        scale = jnp.sqrt(minus_expm1(2.0 * log_a, decay * decay))
        scale = jnp.where(keep > 0.0, scale, 1.0)
        decay = decay * keep
        drive = rows_b.astype(F32) * gate_x * scale
        prods, states = [decay[0:8]], [drive[0:8]]
        for v in range(1, 16):
            step = decay[8 * v : 8 * v + 8]
            prods.append(prods[-1] * step)
            states.append(step * states[-1] + drive[8 * v : 8 * v + 8])
        p, q = prods[-1], states[-1]
        for d in (1, 2, 4):
            inside = sub >= d
            p_before = jnp.where(inside, pltpu.roll(p, d, 0), 1.0)
            q_before = jnp.where(inside, pltpu.roll(q, d, 0), 0.0)
            q = p * q_before + q
            p = p * p_before
        p_in = jnp.where(sub >= 1, pltpu.roll(p, 1, 0), 1.0)
        q_in = jnp.where(sub >= 1, pltpu.roll(q, 1, 0), 0.0)
        comp[0, pl.ds(u, 1), :] = p[7:8]
        comp[1, pl.ds(u, 1), :] = q[7:8]
        for v in range(16):
            prod_b[u, pl.ds(8 * v, 8), :] = prods[v] * p_in
            local_b[u, pl.ds(8 * v, 8), :] = states[v] + prods[v] * q_in
        return 0

    def compute(j):
        lax.fori_loop(0, 4 * SIZES[j], functools.partial(gates, j), 0, unroll=4)

    def mine(j):
        return pl.ds(8 * j, 8)

    def send_row(j):
        rowc[here, :, mine(j), :] = comp[:, mine(j), :]
        src = comp.at[:, mine(j), :]
        for d in range(1, 8):
            to = in_row(lax.rem(here + d, 8))
            remote(src, rowc.at[here, :, mine(j), :], row_s.at[j], row_r.at[j], to).start()

    def direct_copy(j, d):
        k = j - DIRECT
        to = (g, z, lax.rem(s + d, places))
        return remote(comp.at[:, mine(j), :], allc.at[k, s], all_s.at[k, d - 1], all_r.at[k, s], to)

    def send_direct(j):
        for d in range(15, 0, -1):

            @pl.when(s + d < places)
            def _():
                direct_copy(j, d).start()

    def step_direct(j):
        c = j - DIRECT
        for k in range(15):

            @pl.when(k < s)
            def _():
                pltpu.make_async_copy(allc.at[c, k], allc.at[c, k], all_r.at[c, k]).wait()

        entering = jnp.zeros((8, HS), F32)
        for k in range(15):
            through = allc[c, k, 0] * entering + allc[c, k, 1]
            entering = jnp.where(k < s, through, entering)
        inc_b[1, mine(j), :] = entering
        finish_batch(j)

    def seven(j):
        return rowc.at[pl.ds(0, 7), :, mine(j), :]

    def y_copy(j):
        to = (g, z, lax.rem(s + 8, places))
        return remote(tot.at[mine(j)], ysum.at[mine(j)], y_s.at[j], y_r.at[j], to)

    def step_row(j):
        await_bytes(seven(j), row_r.at[j])
        all_p = jnp.zeros((8, HS), F32) + 1.0
        before_p, before_q, all_q = all_p, jnp.zeros((8, HS), F32), jnp.zeros((8, HS), F32)
        for k in range(8):
            a, b = rowc[k, 0, mine(j), :], rowc[k, 1, mine(j), :]
            before_p = jnp.where(k < here, before_p * a, before_p)
            before_q = jnp.where(k < here, a * before_q + b, before_q)
            all_q = a * all_q + b
        tot[mine(j), :] = all_q

        @pl.when(row == 0)
        def _():
            y_copy(j).start()

        inc_b[0, mine(j), :] = before_p
        inc_b[1, mine(j), :] = before_q

    def step_y(j):
        @pl.when(row == 1)
        def _():
            y_copy(j).wait_recv()
            inc_b[1, mine(j), :] = inc_b[0, mine(j), :] * ysum[mine(j), :] + inc_b[1, mine(j), :]

        finish_batch(j)

    def finish_batch(j):
        def finish(index, _):
            u = 8 * j + index
            cols = columns(head_of(j, index))
            entering = inc_b[1, pl.ds(u, 1), :]
            for v in range(16):
                full = local_b[u, pl.ds(8 * v, 8), :] + prod_b[u, pl.ds(8 * v, 8), :] * entering
                tmp[pl.ds(v, 8, stride=16), :] = full
            rounded = tmp[...].astype(BF16)
            student[:, cols] = rounded
            wide = rounded.astype(F32)
            acc_b[...] += wide * wide
            return 0

        lax.fori_loop(0, 4 * SIZES[j], finish, 0, unroll=4)

    def sent(j):
        def by_relay():
            if j:
                for copy in far_copies(j):
                    copy.wait_send()
            await_bytes(wbuf.at[pl.ds(0, 3)] if j == LAST else three(j, 0), near_s.at[j])
            for kind in (0, 3) if j else (3,):
                if j < LAST or kind == 0:
                    await_bytes(three(j, kind), x_s.at[kind, j])
                chip_copy(j, kind).wait_send()

        def by_other():
            for kind in (1, 2):
                if j < LAST:
                    await_bytes(three(j, kind), x_s.at[kind, j])
                chip_copy(j, kind).wait_send()

        both(by_relay, by_other)

    heads = x_v.shape[1] // HS
    lax.fori_loop(0, heads // 2, conv_head, 0, unroll=4)
    step_near(0)
    step_far(1)
    lax.fori_loop(heads // 2, heads, conv_head, 0, unroll=4)
    step_x(0)
    step_far(2)
    step_near(1)
    step_chip(0)
    compute(0)
    send_row(0)
    step_near(2)
    step_x(1)
    step_far(3)
    step_chip(1)
    compute(1)
    send_row(1)
    step_x(2)
    step_far(4)
    step_near(3)
    step_row(0)
    step_chip(2)
    compute(2)
    send_row(2)
    step_x(3)
    step_x(4)
    step_row(1)
    step_y(0)
    step_chip(3)
    compute(3)
    send_direct(3)
    step_row(2)
    step_chip(4)
    compute(4)
    send_direct(4)
    step_y(1)
    for j in range(BATCHES):
        sent(j)
    step_y(2)
    step_direct(3)
    step_direct(4)

    out_copy = pltpu.make_async_copy(student, out_hbm.at[0], out_sem)
    out_copy.start()
    width = x_v.shape[1]
    mean_sq = jnp.sum(acc_b[...], axis=1, keepdims=True) * (1.0 / width)
    tmp[...] = jnp.broadcast_to(lax.rsqrt(mean_sq + 1e-06), (HS, HS))
    for k, block in enumerate(blocks):
        teacher_copies[k].wait_recv()

        def loss_head(head, total):
            cols = columns(head)
            diff = student[block, cols].astype(F32) * tmp[block, :] - tbuf[block, cols].astype(F32)
            return total + diff * diff

        acc_b[block, :] = lax.fori_loop(0, heads, loss_head, jnp.zeros((32, HS), F32), unroll=4)
    loss_ref[...] = jnp.sum(jnp.transpose(acc_b[...]), axis=0, keepdims=True) * (1.0 / width)

    for copy in teacher_copies:
        copy.wait_send()

    @pl.when(s < places - 1)
    def _():
        halo_copy.wait_send()

    @pl.when(row == 0)
    def _():
        for j in range(DIRECT):
            y_copy(j).wait_send()

    for j in range(DIRECT):
        await_bytes(seven(j), row_s.at[j])
    for d in range(1, 16):

        @pl.when(s + d < places)
        def _():
            for j in range(DIRECT, BATCHES):
                direct_copy(j, d).wait_send()

    out_copy.wait()


def local(branch_x, positions, teacher, gate_weights, gate_bias, conv_weight, conv_bias, decay_rate):
    rows, width = branch_x.shape[1:]
    seq_len = rows * lax.axis_size("seq")
    slots = 8 * BATCHES
    dma = pltpu.SemaphoreType.DMA
    operands = (
        branch_x,
        positions,
        teacher,
        gate_weights,
        gate_bias,
        conv_weight,
        conv_bias.reshape(1, width),
        decay_rate.reshape(1, width),
    )
    operands = [pltpu.with_memory_space_constraint(v, pltpu.HBM) for v in operands]
    out, loss = pl.pallas_call(
        functools.partial(kernel, seq_len),
        out_shape=(
            jax.ShapeDtypeStruct((1, rows, width), BF16),
            jax.ShapeDtypeStruct((1, rows), F32),
        ),
        in_specs=[pl.BlockSpec(memory_space=pltpu.HBM)] * 8,
        out_specs=(pl.BlockSpec(memory_space=pltpu.HBM), pl.BlockSpec(memory_space=pltpu.VMEM)),
        scratch_shapes=[
            pltpu.VMEM((rows, width), BF16),
            pltpu.VMEM((16, width), BF16),
            pltpu.VMEM((1, rows), jnp.int32),
            pltpu.VMEM((2, width), F32),
            pltpu.VMEM((4, width), F32),
            pltpu.VMEM((1, width), F32),
            pltpu.VMEM((1, width), F32),
            pltpu.VMEM((rows, width), BF16),
            pltpu.VMEM((slots, 2, HS, HS), BF16),
            pltpu.VMEM((width // HS, rows, HS), BF16),
            pltpu.VMEM((slots, rows, HS), F32),
            pltpu.VMEM((slots, rows, HS), F32),
            pltpu.VMEM((2, slots, HS), F32),
            pltpu.VMEM((8, 2, slots, HS), F32),
            pltpu.VMEM((BATCHES - DIRECT, 16, 2, 8, HS), F32),
            pltpu.VMEM((slots, HS), F32),
            pltpu.VMEM((slots, HS), F32),
            pltpu.VMEM((2, slots, HS), F32),
            pltpu.VMEM((rows + 16, HS), F32),
            pltpu.VMEM((3, rows, HS), F32),
            pltpu.VMEM((rows, HS), F32),
            pltpu.VMEM((rows, HS), F32),
            pltpu.VMEM((rows, width), BF16),
            dma((7,)),
            dma,
            dma((8,)),
            dma((8,)),
            dma((BATCHES,)),
            dma((4, BATCHES)),
            dma((4, BATCHES)),
            dma((4, BATCHES)),
            dma((4, BATCHES)),
            dma((4, BATCHES)),
            dma((BATCHES,)),
            dma((BATCHES,)),
            dma((BATCHES - DIRECT, 15)),
            dma((BATCHES - DIRECT, 16)),
            dma((BATCHES,)),
            dma((BATCHES,)),
            dma((4,)),
            dma((4,)),
            dma,
            dma,
        ],
        compiler_params=pltpu.CompilerParams(
            collective_id=0, has_side_effects=True, vmem_limit_bytes=40 << 20
        ),
        name="step",
    )(*operands)
    return out, loss


def solution(mesh):
    in_specs = (
        P(("segment", "fsdp"), "seq", None),
        P(("segment", "fsdp"), "seq"),
        P(("segment", "fsdp"), "seq", None),
        P("fsdp", None, None, None),
        P(),
        P(),
        P(),
        P(),
    )
    out_specs = (P(("segment", "fsdp"), "seq", None), P(("segment", "fsdp"), "seq"))
    return jax.shard_map(local, mesh=mesh, in_specs=in_specs, out_specs=out_specs, check_vma=False)
```

```python
import functools

import jax
import jax.numpy as jnp
from jax import lax
from jax.experimental import pallas as pl
from jax.experimental.pallas import tpu as pltpu
from jax.sharding import PartitionSpec as P

HS = 128
MESH = pl.DeviceIdType.MESH
F32 = jnp.float32
BF16 = jnp.bfloat16
HEADS_IN = (5, 8, 8, 8, 3)
BATCHES = len(HEADS_IN)
DIRECT = 3


def sigmoid(v):
    return 1.0 / (1.0 + jnp.exp(-v))


def minus_expm1(y, ey):
    series = 1.0 + y * (1 / 2 + y * (1 / 6 + y * (1 / 24 + y * (1 / 120 + y * (1 / 720)))))
    return jnp.where(y > -0.125, -y * series, 1.0 - ey)


def kernel(
    seq_len,
    x_hbm,
    pos_hbm,
    teach_hbm,
    gw_hbm,
    gb_hbm,
    cw_hbm,
    cb_hbm,
    rate_hbm,
    out_hbm,
    loss_ref,
    x_v,
    halo,
    pos_v,
    gb_v,
    cw_v,
    cb_v,
    rate_v,
    tbuf,
    wbuf,
    convb,
    prod_b,
    local_b,
    comp,
    rowc,
    allc,
    tot,
    ysum,
    inc_b,
    xf,
    masks,
    tmp,
    acc_b,
    student,
    load_sem,
    out_sem,
    far_s,
    far_r,
    near_s,
    near_r,
    x_s,
    x_r,
    chip_s,
    chip_r,
    row_s,
    row_r,
    all_s,
    all_r,
    y_s,
    y_r,
    t_s,
    t_r,
    h_s,
    h_r,
):
    g, z, s = lax.axis_index("segment"), lax.axis_index("fsdp"), lax.axis_index("seq")
    planes, places = lax.axis_size("fsdp"), lax.axis_size("seq")
    row, here = s // 8, s % 8
    xc, core = here // 2, s % 2
    relay = lax.rem(z, 2) == core

    def at_z(dz):
        return (g, lax.rem(z + dz + planes, planes), s)

    def in_row(other):
        return (g, z, row * 8 + other)

    def remote(src, dst, send, recv, to):
        return pltpu.make_async_remote_copy(
            src_ref=src, dst_ref=dst, send_sem=send, recv_sem=recv, device_id=to, device_id_type=MESH
        )

    def await_bytes(ref, sem):
        pltpu.make_async_copy(ref, ref, sem).wait()

    loads = [
        pltpu.make_async_copy(gw_hbm.at[0], wbuf.at[0], load_sem.at[0]),
        pltpu.make_async_copy(x_hbm.at[0], x_v, load_sem.at[1]),
        pltpu.make_async_copy(pos_hbm, pos_v, load_sem.at[2]),
        pltpu.make_async_copy(cw_hbm, cw_v, load_sem.at[3]),
        pltpu.make_async_copy(cb_hbm, cb_v, load_sem.at[4]),
        pltpu.make_async_copy(gb_hbm, gb_v, load_sem.at[5]),
        pltpu.make_async_copy(rate_hbm, rate_v, load_sem.at[6]),
    ]
    for copy in loads:
        copy.start()

    partner = (1 - g, z, s)
    other_core = in_row(here // 2 * 2 + 1 - core)
    greeted = [at_z(dz) for dz in (8, -8, 4, -4, 3, -3, 2, -2, 1, -1)]
    greeted += [partner] + [(g, z, lax.rem(s + d, places)) for d in range(1, 16)]
    barrier = pltpu.get_barrier_semaphore()
    for device in greeted:
        pl.semaphore_signal(barrier, inc=1, device_id=device, device_id_type=MESH)
    loads[0].wait()
    pl.semaphore_wait(barrier, len(greeted))

    blocks = [pl.ds(32 * k, 32) for k in range(4)]
    quarter = pl.ds(pl.multiple_of(xc * 32, 32), 32)

    def span(j, kind):
        if j == 0:
            return kind, 2 if kind == 3 else 1
        return (32 + kind, 1) if j == 4 else (8 * j + 2 * kind, 2)

    def kinds(j, by_relay):
        if not by_relay:
            return (1, 2)
        return {0: (3,), 4: (0,)}.get(j, (0, 3))

    def piece(u, count):
        return wbuf.at[pl.ds(u, count), :, quarter, :]

    def far_copy(j, down):
        side = 1 if down else 0
        k = j - 1 + 4 * side
        dz = (4 if j % 2 else 8) * (-1 if down else 1)
        if j == 4:
            gate = pl.ds(side, 1)
            src, dst = (wbuf.at[pl.ds(u, 1), gate, quarter, :] for u in (16 + side, 32))
        else:
            src, dst = piece(16 + side if j == 3 else 0, 1), piece(8 * j + side, 1)
        return remote(src, dst, far_s.at[k], far_r.at[k], at_z(dz))

    def send_near(j):
        def send(u, count, kind, skip, dz, group=j):
            dst = piece(span(group, kind)[0] + skip, count)
            remote(piece(u, count), dst, near_s.at[j], near_r.at[kind, group], at_z(dz)).start()

        u, count = span(j, 0)
        above = u + count - 1
        if j == 3:
            send(above, 1, 1, 0, -3, 4)
            send(u, 1, 2, 0, 3, 4)
        send(u, 1, 3, 0, 2)
        send(above, 1, 3, 1, -2)
        send(u, count, 1, 0, 1)
        send(u, count, 2, 0, -1)

    def near_sent(j):
        return {0: wbuf.at[pl.ds(0, 1)], 3: wbuf.at[pl.ds(0, 2)]}.get(j, three(j, 0))

    def wait_near(j, kind):
        await_bytes(piece(*span(j, kind)), near_r.at[kind, j])

    def send_x(j, kind):
        src = piece(*span(j, kind))
        for d in (2, 1, 3):
            to = in_row(lax.rem(xc + d, 4) * 2 + core)
            remote(src, src, x_s.at[kind, j], x_r.at[kind, j], to).start()

    def three(j, kind):
        return wbuf.at[pl.ds(*span(j, kind)), :, pl.ds(0, 96), :]

    def chip_copy(j, kind):
        src = wbuf.at[pl.ds(*span(j, kind))]
        return remote(src, src, chip_s.at[kind, j], chip_r.at[kind, j], other_core)

    def both(for_relay, for_other):
        @pl.when(relay)
        def _():
            for_relay()

        @pl.when(jnp.logical_not(relay))
        def _():
            for_other()

    def far_copies(j):
        return [far_copy(j, down) for down in (False, True)]

    def start_far(j):
        for copy in far_copies(j):
            copy.start()

    def step_far(j):
        @pl.when(relay)
        def _():
            for copy in far_copies(j):
                copy.wait_recv()
            if j == 2:
                start_far(4)
                start_far(3)
            if j < 4:
                send_near(j)
            send_x(j, 0)

    def step_near(j):
        def get(by_relay):
            for kind in kinds(j, by_relay):
                if kind:
                    wait_near(j, kind)
                    send_x(j, kind)

        both(functools.partial(get, True), functools.partial(get, False))

    def step_x(j):
        def hand_over(by_relay):
            for kind in kinds(j, by_relay):
                await_bytes(three(j, kind), x_r.at[kind, j])
                chip_copy(j, kind).start()

        both(functools.partial(hand_over, True), functools.partial(hand_over, False))

    def step_chip(j):
        def get(by_relay):
            for kind in kinds(j, not by_relay):
                chip_copy(j, kind).wait_recv()

        both(functools.partial(get, True), functools.partial(get, False))

    @pl.when(relay)
    def _():
        start_far(2)
        start_far(1)
        send_near(0)

    halo_copy = remote(x_hbm.at[0, pl.ds(112, 16), :], halo, h_s, h_r, (g, z, lax.rem(s + 1, places)))
    teacher_copies = [
        remote(teach_hbm.at[0, block, :], tbuf.at[block, :], t_s.at[k], t_r.at[k], partner)
        for k, block in enumerate(blocks)
    ]

    @pl.when(s < places - 1)
    def _():
        halo_copy.start()

    for copy in teacher_copies:
        copy.start()
    for copy in loads[1:]:
        copy.wait()

    pos = jnp.transpose(jnp.broadcast_to(pos_v[...].astype(F32), (HS, HS)))
    tmp[...] = pos
    for v in range(16):
        places_v = tmp[pl.ds(v, 8, stride=16), :]
        for k in range(3):
            masks[k, pl.ds(8 * v, 8), :] = (places_v >= k + 1.0).astype(F32)
    comp[...] = jnp.zeros_like(comp)
    acc_b[...] = jnp.zeros_like(acc_b)

    def columns(head):
        return pl.ds(pl.multiple_of(head * HS, HS), HS)

    @pl.when(s > 0)
    def _():
        halo_copy.wait_recv()

    @pl.when(s == 0)
    def _():
        halo[...] = jnp.zeros_like(halo)

    def conv_head(head, _):
        cols = columns(head)
        xf[pl.ds(0, 16), :] = halo[:, cols].astype(F32)
        xf[pl.ds(16, HS), :] = x_v[:, cols].astype(F32)
        rows = {v: xf[pl.ds(16 + v, 8, stride=16), :] for v in range(-3, 16)}
        taps = [cw_v[pl.ds(k, 1), cols] for k in range(4)]
        bias = cb_v[:, cols]
        out = []
        for v in range(16):
            total = bias + taps[0] * rows[v]
            for k in range(1, 4):
                total = total + taps[k] * rows[v - k] * masks[k - 1, pl.ds(8 * v, 8), :]
            out.append(total)
        convb[head] = jnp.concatenate(out, axis=0).astype(BF16)
        return 0

    def head_of(j, index):
        if j in (0, 4):
            away = jnp.int32(0)
            for k, dz in enumerate((0, -1, 1, -2, 2) if j == 0 else (16, 15, -15)):
                away = jnp.where(index == k, dz, away)
        else:
            kind, side = index // 2, index % 2
            side = 2 * side - 1
            near = jnp.where(kind == 0, 0, jnp.where(kind == 1, -1, jnp.where(kind == 2, 1, 2 * side)))
            away = near + 4 * j * side
        return lax.rem(z + away + planes, planes)

    sub = lax.broadcasted_iota(jnp.int32, (8, HS), 0)

    def gates(j, index, _):
        u = 8 * j + index
        head = head_of(j, index)
        cols = columns(head)
        rows_b = convb[head]
        pre_x = jnp.dot(rows_b, wbuf[u, 0], preferred_element_type=F32)
        pre_a = jnp.dot(rows_b, wbuf[u, 1], preferred_element_type=F32)
        gate_x = sigmoid(pre_x + gb_v[pl.ds(0, 1), cols])
        gate_a = sigmoid(pre_a + gb_v[pl.ds(1, 1), cols])
        log_a = gate_a * (rate_v[:, cols] * (-8.0 / seq_len))
        keep = masks[0]
        decay = jnp.exp(log_a)
        scale = jnp.sqrt(minus_expm1(2.0 * log_a, decay * decay))
        scale = jnp.where(keep > 0.0, scale, 1.0)
        decay = decay * keep
        drive = rows_b.astype(F32) * gate_x * scale
        prods, states = [decay[0:8]], [drive[0:8]]
        for v in range(1, 16):
            step = decay[8 * v : 8 * v + 8]
            prods.append(prods[-1] * step)
            states.append(step * states[-1] + drive[8 * v : 8 * v + 8])
        p, q = prods[-1], states[-1]
        for d in (1, 2, 4):
            inside = sub >= d
            p_before = jnp.where(inside, pltpu.roll(p, d, 0), 1.0)
            q_before = jnp.where(inside, pltpu.roll(q, d, 0), 0.0)
            q = p * q_before + q
            p = p * p_before
        p_in = jnp.where(sub >= 1, pltpu.roll(p, 1, 0), 1.0)
        q_in = jnp.where(sub >= 1, pltpu.roll(q, 1, 0), 0.0)
        comp[0, pl.ds(u, 1), :] = p[7:8]
        comp[1, pl.ds(u, 1), :] = q[7:8]
        for v in range(16):
            prod_b[u, pl.ds(8 * v, 8), :] = prods[v] * p_in
            local_b[u, pl.ds(8 * v, 8), :] = states[v] + prods[v] * q_in
        return 0

    def compute(j):
        unroll = HEADS_IN[j] if HEADS_IN[j] < 8 else 4
        lax.fori_loop(0, HEADS_IN[j], functools.partial(gates, j), 0, unroll=unroll)

    def mine(j):
        return pl.ds(8 * j, 8)

    def send_row(j):
        rowc[here, :, mine(j), :] = comp[:, mine(j), :]
        src = comp.at[:, mine(j), :]
        for d in range(1, 8):
            to = in_row(lax.rem(here + d, 8))
            remote(src, rowc.at[here, :, mine(j), :], row_s.at[j], row_r.at[j], to).start()

    def direct_copy(j, d):
        k = j - DIRECT
        to = (g, z, lax.rem(s + d, places))
        return remote(comp.at[:, mine(j), :], allc.at[k, s], all_s.at[k, d - 1], all_r.at[k, s], to)

    def send_direct(j):
        for d in range(15, 0, -1):

            @pl.when(s + d < places)
            def _():
                direct_copy(j, d).start()

    def step_direct(j):
        c = j - DIRECT
        for k in range(15):

            @pl.when(k < s)
            def _():
                pltpu.make_async_copy(allc.at[c, k], allc.at[c, k], all_r.at[c, k]).wait()

        entering = jnp.zeros((8, HS), F32)
        for k in range(15):
            through = allc[c, k, 0] * entering + allc[c, k, 1]
            entering = jnp.where(k < s, through, entering)
        inc_b[1, mine(j), :] = entering
        finish_batch(j)

    def seven(j):
        return rowc.at[pl.ds(0, 7), :, mine(j), :]

    def y_copy(j):
        to = (g, z, lax.rem(s + 8, places))
        return remote(tot.at[mine(j)], ysum.at[mine(j)], y_s.at[j], y_r.at[j], to)

    def step_row(j):
        await_bytes(seven(j), row_r.at[j])
        all_p = jnp.zeros((8, HS), F32) + 1.0
        before_p, before_q, all_q = all_p, jnp.zeros((8, HS), F32), jnp.zeros((8, HS), F32)
        for k in range(8):
            a, b = rowc[k, 0, mine(j), :], rowc[k, 1, mine(j), :]
            before_p = jnp.where(k < here, before_p * a, before_p)
            before_q = jnp.where(k < here, a * before_q + b, before_q)
            all_q = a * all_q + b
        tot[mine(j), :] = all_q

        @pl.when(row == 0)
        def _():
            y_copy(j).start()

        inc_b[0, mine(j), :] = before_p
        inc_b[1, mine(j), :] = before_q

    def step_y(j):
        @pl.when(row == 1)
        def _():
            y_copy(j).wait_recv()
            inc_b[1, mine(j), :] = inc_b[0, mine(j), :] * ysum[mine(j), :] + inc_b[1, mine(j), :]

        finish_batch(j)

    def finish_batch(j):
        def finish(index, _):
            u = 8 * j + index
            cols = columns(head_of(j, index))
            entering = inc_b[1, pl.ds(u, 1), :]
            for v in range(16):
                full = local_b[u, pl.ds(8 * v, 8), :] + prod_b[u, pl.ds(8 * v, 8), :] * entering
                tmp[pl.ds(v, 8, stride=16), :] = full
            rounded = tmp[...].astype(BF16)
            student[:, cols] = rounded
            wide = rounded.astype(F32)
            acc_b[...] += wide * wide
            return 0

        unroll = HEADS_IN[j] if HEADS_IN[j] < 8 else 4
        lax.fori_loop(0, HEADS_IN[j], finish, 0, unroll=unroll)

    def sent(j):
        def clear(by_relay):
            if by_relay and j:
                for copy in far_copies(j):
                    copy.wait_send()
            if by_relay and j < 4:
                await_bytes(near_sent(j), near_s.at[j])
            for kind in kinds(j, by_relay):
                await_bytes(three(j, kind), x_s.at[kind, j])
                chip_copy(j, kind).wait_send()

        both(functools.partial(clear, True), functools.partial(clear, False))

    heads = x_v.shape[1] // HS
    lax.fori_loop(0, heads // 2, conv_head, 0, unroll=4)
    step_near(0)
    step_far(1)
    step_far(2)
    lax.fori_loop(heads // 2, heads, conv_head, 0, unroll=4)
    step_x(0)
    step_near(1)
    step_chip(0)
    compute(0)
    send_row(0)
    step_near(2)
    step_x(1)
    step_far(3)
    step_chip(1)
    compute(1)
    send_row(1)
    step_row(0)
    step_far(4)
    step_x(2)
    step_near(3)
    step_near(4)
    step_chip(2)
    compute(2)
    send_row(2)
    step_x(3)
    step_x(4)
    step_row(1)
    step_y(0)
    step_chip(3)
    compute(3)
    send_direct(3)
    step_row(2)
    step_chip(4)
    compute(4)
    send_direct(4)
    step_y(1)
    for j in range(BATCHES):
        sent(j)
    step_y(2)
    step_direct(3)
    step_direct(4)

    out_copy = pltpu.make_async_copy(student, out_hbm.at[0], out_sem)
    out_copy.start()
    width = x_v.shape[1]
    mean_sq = jnp.sum(acc_b[...], axis=1, keepdims=True) * (1.0 / width)
    tmp[...] = jnp.broadcast_to(lax.rsqrt(mean_sq + 1e-06), (HS, HS))
    for k, block in enumerate(blocks):
        teacher_copies[k].wait_recv()

        def loss_head(head, total):
            cols = columns(head)
            diff = student[block, cols].astype(F32) * tmp[block, :] - tbuf[block, cols].astype(F32)
            return total + diff * diff

        acc_b[block, :] = lax.fori_loop(0, heads, loss_head, jnp.zeros((32, HS), F32), unroll=4)
    loss_ref[...] = jnp.sum(jnp.transpose(acc_b[...]), axis=0, keepdims=True) * (1.0 / width)

    for copy in teacher_copies:
        copy.wait_send()

    @pl.when(s < places - 1)
    def _():
        halo_copy.wait_send()

    @pl.when(row == 0)
    def _():
        for j in range(DIRECT):
            y_copy(j).wait_send()

    for j in range(DIRECT):
        await_bytes(seven(j), row_s.at[j])
    for d in range(1, 16):

        @pl.when(s + d < places)
        def _():
            for j in range(DIRECT, BATCHES):
                direct_copy(j, d).wait_send()

    out_copy.wait()


def local(branch_x, positions, teacher, gate_weights, gate_bias, conv_weight, conv_bias, decay_rate):
    rows, width = branch_x.shape[1:]
    seq_len = rows * lax.axis_size("seq")
    slots = 8 * BATCHES
    dma = pltpu.SemaphoreType.DMA
    operands = (
        branch_x,
        positions,
        teacher,
        gate_weights,
        gate_bias,
        conv_weight,
        conv_bias.reshape(1, width),
        decay_rate.reshape(1, width),
    )
    operands = [pltpu.with_memory_space_constraint(v, pltpu.HBM) for v in operands]
    out, loss = pl.pallas_call(
        functools.partial(kernel, seq_len),
        out_shape=(
            jax.ShapeDtypeStruct((1, rows, width), BF16),
            jax.ShapeDtypeStruct((1, rows), F32),
        ),
        in_specs=[pl.BlockSpec(memory_space=pltpu.HBM)] * 8,
        out_specs=(pl.BlockSpec(memory_space=pltpu.HBM), pl.BlockSpec(memory_space=pltpu.VMEM)),
        scratch_shapes=[
            pltpu.VMEM((rows, width), BF16),
            pltpu.VMEM((16, width), BF16),
            pltpu.VMEM((1, rows), jnp.int32),
            pltpu.VMEM((2, width), F32),
            pltpu.VMEM((4, width), F32),
            pltpu.VMEM((1, width), F32),
            pltpu.VMEM((1, width), F32),
            pltpu.VMEM((rows, width), BF16),
            pltpu.VMEM((slots, 2, HS, HS), BF16),
            pltpu.VMEM((width // HS, rows, HS), BF16),
            pltpu.VMEM((slots, rows, HS), F32),
            pltpu.VMEM((slots, rows, HS), F32),
            pltpu.VMEM((2, slots, HS), F32),
            pltpu.VMEM((8, 2, slots, HS), F32),
            pltpu.VMEM((BATCHES - DIRECT, 16, 2, 8, HS), F32),
            pltpu.VMEM((slots, HS), F32),
            pltpu.VMEM((slots, HS), F32),
            pltpu.VMEM((2, slots, HS), F32),
            pltpu.VMEM((rows + 16, HS), F32),
            pltpu.VMEM((3, rows, HS), F32),
            pltpu.VMEM((rows, HS), F32),
            pltpu.VMEM((rows, HS), F32),
            pltpu.VMEM((rows, width), BF16),
            dma((7,)),
            dma,
            dma((8,)),
            dma((8,)),
            dma((BATCHES,)),
            dma((4, BATCHES)),
            dma((4, BATCHES)),
            dma((4, BATCHES)),
            dma((4, BATCHES)),
            dma((4, BATCHES)),
            dma((BATCHES,)),
            dma((BATCHES,)),
            dma((BATCHES - DIRECT, 15)),
            dma((BATCHES - DIRECT, 16)),
            dma((BATCHES,)),
            dma((BATCHES,)),
            dma((4,)),
            dma((4,)),
            dma,
            dma,
        ],
        compiler_params=pltpu.CompilerParams(
            collective_id=0, has_side_effects=True, vmem_limit_bytes=40 << 20
        ),
        name="step",
    )(*operands)
    return out, loss


def solution(mesh):
    in_specs = (
        P(("segment", "fsdp"), "seq", None),
        P(("segment", "fsdp"), "seq"),
        P(("segment", "fsdp"), "seq", None),
        P("fsdp", None, None, None),
        P(),
        P(),
        P(),
        P(),
    )
    out_specs = (P(("segment", "fsdp"), "seq", None), P(("segment", "fsdp"), "seq"))
    return jax.shard_map(local, mesh=mesh, in_specs=in_specs, out_specs=out_specs, check_vma=False)
```

```python
import functools

import jax
import jax.numpy as jnp
from jax import lax
from jax.experimental import pallas as pl
from jax.experimental.pallas import tpu as pltpu
from jax.sharding import PartitionSpec as P

HS = 128
MESH = pl.DeviceIdType.MESH
F32 = jnp.float32
BF16 = jnp.bfloat16
HEADS_IN = (5, 8, 8, 8, 3)
BATCHES = len(HEADS_IN)
DIRECT = 3


def sigmoid(v):
    return 1.0 / (1.0 + jnp.exp(-v))


def minus_expm1(y, ey):
    series = 1.0 + y * (1 / 2 + y * (1 / 6 + y * (1 / 24 + y * (1 / 120 + y * (1 / 720)))))
    return jnp.where(y > -0.125, -y * series, 1.0 - ey)


def kernel(
    seq_len,
    x_hbm,
    pos_hbm,
    teach_hbm,
    gw_hbm,
    gb_hbm,
    cw_hbm,
    cb_hbm,
    rate_hbm,
    student,
    tbuf,
    norm_ref,
    x_v,
    halo,
    pos_v,
    gb_v,
    cw_v,
    cb_v,
    rate_v,
    wbuf,
    convb,
    prod_b,
    local_b,
    comp,
    rowc,
    allc,
    tot,
    ysum,
    inc_b,
    xf,
    masks,
    tmp,
    acc_b,
    load_sem,
    far_s,
    far_r,
    near_s,
    near_r,
    x_s,
    x_r,
    chip_s,
    chip_r,
    row_s,
    row_r,
    all_s,
    all_r,
    y_s,
    y_r,
    t_s,
    t_r,
    h_s,
    h_r,
):
    g, z, s = lax.axis_index("segment"), lax.axis_index("fsdp"), lax.axis_index("seq")
    planes, places = lax.axis_size("fsdp"), lax.axis_size("seq")
    row, here = s // 8, s % 8
    xc, core = here // 2, s % 2
    relay = lax.rem(z, 2) == core

    def at_z(dz):
        return (g, lax.rem(z + dz + planes, planes), s)

    def in_row(other):
        return (g, z, row * 8 + other)

    def remote(src, dst, send, recv, to):
        return pltpu.make_async_remote_copy(
            src_ref=src, dst_ref=dst, send_sem=send, recv_sem=recv, device_id=to, device_id_type=MESH
        )

    def await_bytes(ref, sem):
        pltpu.make_async_copy(ref, ref, sem).wait()

    loads = [
        pltpu.make_async_copy(gw_hbm.at[0], wbuf.at[0], load_sem.at[0]),
        pltpu.make_async_copy(x_hbm.at[0], x_v, load_sem.at[1]),
        pltpu.make_async_copy(pos_hbm, pos_v, load_sem.at[2]),
        pltpu.make_async_copy(cw_hbm, cw_v, load_sem.at[3]),
        pltpu.make_async_copy(cb_hbm, cb_v, load_sem.at[4]),
        pltpu.make_async_copy(gb_hbm, gb_v, load_sem.at[5]),
        pltpu.make_async_copy(rate_hbm, rate_v, load_sem.at[6]),
    ]
    for copy in loads:
        copy.start()

    partner = (1 - g, z, s)
    other_core = in_row(here // 2 * 2 + 1 - core)
    greeted = [at_z(dz) for dz in (8, -8, 4, -4, 3, -3, 2, -2, 1, -1)]
    greeted += [partner] + [(g, z, lax.rem(s + d, places)) for d in range(1, 16)]
    barrier = pltpu.get_barrier_semaphore()
    for device in greeted:
        pl.semaphore_signal(barrier, inc=1, device_id=device, device_id_type=MESH)
    loads[0].wait()
    pl.semaphore_wait(barrier, len(greeted))

    blocks = [pl.ds(32 * k, 32) for k in range(4)]
    quarter = pl.ds(pl.multiple_of(xc * 32, 32), 32)

    def span(j, kind):
        if j == 0:
            return kind, 2 if kind == 3 else 1
        return (32 + kind, 1) if j == 4 else (8 * j + 2 * kind, 2)

    def kinds(j, by_relay):
        if not by_relay:
            return (1, 2)
        return {0: (3,), 4: (0,)}.get(j, (0, 3))

    def piece(u, count):
        return wbuf.at[pl.ds(u, count), :, quarter, :]

    def far_copy(j, down):
        side = 1 if down else 0
        k = j - 1 + 4 * side
        dz = (4 if j % 2 else 8) * (-1 if down else 1)
        if j == 4:
            gate = pl.ds(side, 1)
            src, dst = (wbuf.at[pl.ds(u, 1), gate, quarter, :] for u in (16 + side, 32))
        else:
            src, dst = piece(16 + side if j == 3 else 0, 1), piece(8 * j + side, 1)
        return remote(src, dst, far_s.at[k], far_r.at[k], at_z(dz))

    def send_near(j):
        def send(u, count, kind, skip, dz, group=j):
            dst = piece(span(group, kind)[0] + skip, count)
            remote(piece(u, count), dst, near_s.at[j], near_r.at[kind, group], at_z(dz)).start()

        u, count = span(j, 0)
        above = u + count - 1
        if j == 3:
            send(above, 1, 1, 0, -3, 4)
            send(u, 1, 2, 0, 3, 4)
        send(u, 1, 3, 0, 2)
        send(above, 1, 3, 1, -2)
        send(u, count, 1, 0, 1)
        send(u, count, 2, 0, -1)

    def near_sent(j):
        return {0: wbuf.at[pl.ds(0, 1)], 3: wbuf.at[pl.ds(0, 2)]}.get(j, three(j, 0))

    def wait_near(j, kind):
        await_bytes(piece(*span(j, kind)), near_r.at[kind, j])

    def send_x(j, kind):
        src = piece(*span(j, kind))
        for d in (2, 1, 3):
            to = in_row(lax.rem(xc + d, 4) * 2 + core)
            remote(src, src, x_s.at[kind, j], x_r.at[kind, j], to).start()

    def three(j, kind):
        return wbuf.at[pl.ds(*span(j, kind)), :, pl.ds(0, 96), :]

    def chip_copy(j, kind):
        src = wbuf.at[pl.ds(*span(j, kind))]
        return remote(src, src, chip_s.at[kind, j], chip_r.at[kind, j], other_core)

    def both(for_relay, for_other):
        @pl.when(relay)
        def _():
            for_relay()

        @pl.when(jnp.logical_not(relay))
        def _():
            for_other()

    def far_copies(j):
        return [far_copy(j, down) for down in (False, True)]

    def start_far(j):
        for copy in far_copies(j):
            copy.start()

    def step_far(j):
        @pl.when(relay)
        def _():
            for copy in far_copies(j):
                copy.wait_recv()
            if j == 2:
                start_far(4)
                start_far(3)
            if j < 4:
                send_near(j)
            send_x(j, 0)

    def step_near(j):
        def get(by_relay):
            for kind in kinds(j, by_relay):
                if kind:
                    wait_near(j, kind)
                    send_x(j, kind)

        both(functools.partial(get, True), functools.partial(get, False))

    def step_x(j):
        def hand_over(by_relay):
            for kind in kinds(j, by_relay):
                await_bytes(three(j, kind), x_r.at[kind, j])
                chip_copy(j, kind).start()

        both(functools.partial(hand_over, True), functools.partial(hand_over, False))

    def step_chip(j):
        def get(by_relay):
            for kind in kinds(j, not by_relay):
                chip_copy(j, kind).wait_recv()

        both(functools.partial(get, True), functools.partial(get, False))

    @pl.when(relay)
    def _():
        start_far(2)
        start_far(1)
        send_near(0)

    halo_copy = remote(x_hbm.at[0, pl.ds(112, 16), :], halo, h_s, h_r, (g, z, lax.rem(s + 1, places)))
    teacher_copies = [
        remote(teach_hbm.at[0, block, :], tbuf.at[block, :], t_s.at[k], t_r.at[k], partner)
        for k, block in enumerate(blocks)
    ]

    @pl.when(s < places - 1)
    def _():
        halo_copy.start()

    for copy in teacher_copies:
        copy.start()
    for copy in loads[1:]:
        copy.wait()

    pos = jnp.transpose(jnp.broadcast_to(pos_v[...].astype(F32), (HS, HS)))
    tmp[...] = pos
    for v in range(16):
        places_v = tmp[pl.ds(v, 8, stride=16), :]
        for k in range(3):
            masks[k, pl.ds(8 * v, 8), :] = (places_v >= k + 1.0).astype(F32)
    comp[...] = jnp.zeros_like(comp)
    acc_b[...] = jnp.zeros_like(acc_b)

    def columns(head):
        return pl.ds(pl.multiple_of(head * HS, HS), HS)

    @pl.when(s > 0)
    def _():
        halo_copy.wait_recv()

    @pl.when(s == 0)
    def _():
        halo[...] = jnp.zeros_like(halo)

    def conv_head(head, _):
        cols = columns(head)
        xf[pl.ds(0, 16), :] = halo[:, cols].astype(F32)
        xf[pl.ds(16, HS), :] = x_v[:, cols].astype(F32)
        rows = {v: xf[pl.ds(16 + v, 8, stride=16), :] for v in range(-3, 16)}
        taps = [cw_v[pl.ds(k, 1), cols] for k in range(4)]
        bias = cb_v[:, cols]
        out = []
        for v in range(16):
            total = bias + taps[0] * rows[v]
            for k in range(1, 4):
                total = total + taps[k] * rows[v - k] * masks[k - 1, pl.ds(8 * v, 8), :]
            out.append(total)
        convb[head] = jnp.concatenate(out, axis=0).astype(BF16)
        return 0

    def head_of(j, index):
        if j in (0, 4):
            away = jnp.int32(0)
            for k, dz in enumerate((0, -1, 1, -2, 2) if j == 0 else (16, 15, -15)):
                away = jnp.where(index == k, dz, away)
        else:
            kind, side = index // 2, index % 2
            side = 2 * side - 1
            near = jnp.where(kind == 0, 0, jnp.where(kind == 1, -1, jnp.where(kind == 2, 1, 2 * side)))
            away = near + 4 * j * side
        return lax.rem(z + away + planes, planes)

    sub = lax.broadcasted_iota(jnp.int32, (8, HS), 0)

    def gates(j, index, _):
        u = 8 * j + index
        head = head_of(j, index)
        cols = columns(head)
        rows_b = convb[head]
        pre_x = jnp.dot(rows_b, wbuf[u, 0], preferred_element_type=F32)
        pre_a = jnp.dot(rows_b, wbuf[u, 1], preferred_element_type=F32)
        gate_x = sigmoid(pre_x + gb_v[pl.ds(0, 1), cols])
        gate_a = sigmoid(pre_a + gb_v[pl.ds(1, 1), cols])
        log_a = gate_a * (rate_v[:, cols] * (-8.0 / seq_len))
        keep = masks[0]
        decay = jnp.exp(log_a)
        scale = jnp.sqrt(minus_expm1(2.0 * log_a, decay * decay))
        scale = jnp.where(keep > 0.0, scale, 1.0)
        decay = decay * keep
        drive = rows_b.astype(F32) * gate_x * scale
        prods, states = [decay[0:8]], [drive[0:8]]
        for v in range(1, 16):
            step = decay[8 * v : 8 * v + 8]
            prods.append(prods[-1] * step)
            states.append(step * states[-1] + drive[8 * v : 8 * v + 8])
        p, q = prods[-1], states[-1]
        for d in (1, 2, 4):
            inside = sub >= d
            p_before = jnp.where(inside, pltpu.roll(p, d, 0), 1.0)
            q_before = jnp.where(inside, pltpu.roll(q, d, 0), 0.0)
            q = p * q_before + q
            p = p * p_before
        p_in = jnp.where(sub >= 1, pltpu.roll(p, 1, 0), 1.0)
        q_in = jnp.where(sub >= 1, pltpu.roll(q, 1, 0), 0.0)
        comp[0, pl.ds(u, 1), :] = p[7:8]
        comp[1, pl.ds(u, 1), :] = q[7:8]
        for v in range(16):
            prod_b[u, pl.ds(8 * v, 8), :] = prods[v] * p_in
            local_b[u, pl.ds(8 * v, 8), :] = states[v] + prods[v] * q_in
        return 0

    def compute(j):
        unroll = HEADS_IN[j] if HEADS_IN[j] < 8 else 4
        lax.fori_loop(0, HEADS_IN[j], functools.partial(gates, j), 0, unroll=unroll)

    def mine(j):
        return pl.ds(8 * j, 8)

    def send_row(j):
        rowc[here, :, mine(j), :] = comp[:, mine(j), :]
        src = comp.at[:, mine(j), :]
        for d in range(1, 8):
            to = in_row(lax.rem(here + d, 8))
            remote(src, rowc.at[here, :, mine(j), :], row_s.at[j], row_r.at[j], to).start()

    def direct_copy(j, d):
        k = j - DIRECT
        to = (g, z, lax.rem(s + d, places))
        return remote(comp.at[:, mine(j), :], allc.at[k, s], all_s.at[k, d - 1], all_r.at[k, s], to)

    def send_direct(j):
        for d in range(15, 0, -1):

            @pl.when(s + d < places)
            def _():
                direct_copy(j, d).start()

    def step_direct(j):
        c = j - DIRECT
        for k in range(15):

            @pl.when(k < s)
            def _():
                pltpu.make_async_copy(allc.at[c, k], allc.at[c, k], all_r.at[c, k]).wait()

        entering = jnp.zeros((8, HS), F32)
        for k in range(15):
            through = allc[c, k, 0] * entering + allc[c, k, 1]
            entering = jnp.where(k < s, through, entering)
        inc_b[1, mine(j), :] = entering
        finish_batch(j)

    def seven(j):
        return rowc.at[pl.ds(0, 7), :, mine(j), :]

    def y_copy(j):
        to = (g, z, lax.rem(s + 8, places))
        return remote(tot.at[mine(j)], ysum.at[mine(j)], y_s.at[j], y_r.at[j], to)

    def step_row(j):
        await_bytes(seven(j), row_r.at[j])
        all_p = jnp.zeros((8, HS), F32) + 1.0
        before_p, before_q, all_q = all_p, jnp.zeros((8, HS), F32), jnp.zeros((8, HS), F32)
        for k in range(8):
            a, b = rowc[k, 0, mine(j), :], rowc[k, 1, mine(j), :]
            before_p = jnp.where(k < here, before_p * a, before_p)
            before_q = jnp.where(k < here, a * before_q + b, before_q)
            all_q = a * all_q + b
        tot[mine(j), :] = all_q

        @pl.when(row == 0)
        def _():
            y_copy(j).start()

        inc_b[0, mine(j), :] = before_p
        inc_b[1, mine(j), :] = before_q

    def step_y(j):
        @pl.when(row == 1)
        def _():
            y_copy(j).wait_recv()
            inc_b[1, mine(j), :] = inc_b[0, mine(j), :] * ysum[mine(j), :] + inc_b[1, mine(j), :]

        finish_batch(j)

    def finish_batch(j):
        def finish(index, _):
            u = 8 * j + index
            cols = columns(head_of(j, index))
            entering = inc_b[1, pl.ds(u, 1), :]
            for v in range(16):
                full = local_b[u, pl.ds(8 * v, 8), :] + prod_b[u, pl.ds(8 * v, 8), :] * entering
                tmp[pl.ds(v, 8, stride=16), :] = full
            rounded = tmp[...].astype(BF16)
            student[:, cols] = rounded
            wide = rounded.astype(F32)
            acc_b[...] += wide * wide
            return 0

        unroll = HEADS_IN[j] if HEADS_IN[j] < 8 else 4
        lax.fori_loop(0, HEADS_IN[j], finish, 0, unroll=unroll)

    def sent(j):
        def clear(by_relay):
            if by_relay and j:
                for copy in far_copies(j):
                    copy.wait_send()
            if by_relay and j < 4:
                await_bytes(near_sent(j), near_s.at[j])
            for kind in kinds(j, by_relay):
                await_bytes(three(j, kind), x_s.at[kind, j])
                chip_copy(j, kind).wait_send()

        both(functools.partial(clear, True), functools.partial(clear, False))

    heads = x_v.shape[1] // HS
    lax.fori_loop(0, heads // 2, conv_head, 0, unroll=4)
    step_near(0)
    step_far(1)
    step_far(2)
    lax.fori_loop(heads // 2, heads, conv_head, 0, unroll=4)
    step_x(0)
    step_near(1)
    step_chip(0)
    compute(0)
    send_row(0)
    step_near(2)
    step_x(1)
    step_far(3)
    step_chip(1)
    compute(1)
    send_row(1)
    step_row(0)
    step_far(4)
    step_x(2)
    step_near(3)
    step_near(4)
    step_chip(2)
    compute(2)
    send_row(2)
    step_x(3)
    step_x(4)
    step_row(1)
    step_y(0)
    step_chip(3)
    compute(3)
    send_direct(3)
    step_row(2)
    step_chip(4)
    compute(4)
    send_direct(4)
    step_y(1)
    for j in range(BATCHES):
        sent(j)
    step_y(2)
    step_direct(3)
    step_direct(4)

    mean_sq = jnp.sum(acc_b[...], axis=1, keepdims=True) * (1.0 / x_v.shape[1])
    norm_ref[...] = jnp.broadcast_to(lax.rsqrt(mean_sq + 1e-06), (HS, HS))
    for copy in teacher_copies:
        copy.wait_recv()

    for copy in teacher_copies:
        copy.wait_send()

    @pl.when(s < places - 1)
    def _():
        halo_copy.wait_send()

    @pl.when(row == 0)
    def _():
        for j in range(DIRECT):
            y_copy(j).wait_send()

    for j in range(DIRECT):
        await_bytes(seven(j), row_s.at[j])
    for d in range(1, 16):

        @pl.when(s + d < places)
        def _():
            for j in range(DIRECT, BATCHES):
                direct_copy(j, d).wait_send()


def finish_kernel(student, target, norm_ref, out_hbm, loss_ref, acc_b, out_sem):
    out_copy = pltpu.make_async_copy(student, out_hbm.at[0], out_sem)
    out_copy.start()
    width = student.shape[1]
    for k in range(4):
        block = pl.ds(32 * k, 32)

        def loss_head(head, total):
            cols = pl.ds(pl.multiple_of(head * HS, HS), HS)
            diff = student[block, cols].astype(F32) * norm_ref[block, :] - target[block, cols].astype(F32)
            return total + diff * diff

        zero = jnp.zeros((32, HS), F32)
        acc_b[block, :] = lax.fori_loop(0, width // HS, loss_head, zero, unroll=8)
    loss_ref[...] = jnp.sum(jnp.transpose(acc_b[...]), axis=0, keepdims=True) * (1.0 / width)
    out_copy.wait()


def local(branch_x, positions, teacher, gate_weights, gate_bias, conv_weight, conv_bias, decay_rate):
    rows, width = branch_x.shape[1:]
    seq_len = rows * lax.axis_size("seq")
    slots = 8 * BATCHES
    dma = pltpu.SemaphoreType.DMA
    operands = (
        branch_x,
        positions,
        teacher,
        gate_weights,
        gate_bias,
        conv_weight,
        conv_bias.reshape(1, width),
        decay_rate.reshape(1, width),
    )
    operands = [pltpu.with_memory_space_constraint(v, pltpu.HBM) for v in operands]
    held = pl.pallas_call(
        functools.partial(kernel, seq_len),
        out_shape=(
            jax.ShapeDtypeStruct((rows, width), BF16),
            jax.ShapeDtypeStruct((rows, width), BF16),
            jax.ShapeDtypeStruct((rows, HS), F32),
        ),
        in_specs=[pl.BlockSpec(memory_space=pltpu.HBM)] * 8,
        out_specs=[pl.BlockSpec(memory_space=pltpu.VMEM)] * 3,
        scratch_shapes=[
            pltpu.VMEM((rows, width), BF16),
            pltpu.VMEM((16, width), BF16),
            pltpu.VMEM((1, rows), jnp.int32),
            pltpu.VMEM((2, width), F32),
            pltpu.VMEM((4, width), F32),
            pltpu.VMEM((1, width), F32),
            pltpu.VMEM((1, width), F32),
            pltpu.VMEM((slots, 2, HS, HS), BF16),
            pltpu.VMEM((width // HS, rows, HS), BF16),
            pltpu.VMEM((slots, rows, HS), F32),
            pltpu.VMEM((slots, rows, HS), F32),
            pltpu.VMEM((2, slots, HS), F32),
            pltpu.VMEM((8, 2, slots, HS), F32),
            pltpu.VMEM((BATCHES - DIRECT, 16, 2, 8, HS), F32),
            pltpu.VMEM((slots, HS), F32),
            pltpu.VMEM((slots, HS), F32),
            pltpu.VMEM((2, slots, HS), F32),
            pltpu.VMEM((rows + 16, HS), F32),
            pltpu.VMEM((3, rows, HS), F32),
            pltpu.VMEM((rows, HS), F32),
            pltpu.VMEM((rows, HS), F32),
            dma((7,)),
            dma((8,)),
            dma((8,)),
            dma((BATCHES,)),
            dma((4, BATCHES)),
            dma((4, BATCHES)),
            dma((4, BATCHES)),
            dma((4, BATCHES)),
            dma((4, BATCHES)),
            dma((BATCHES,)),
            dma((BATCHES,)),
            dma((BATCHES - DIRECT, 15)),
            dma((BATCHES - DIRECT, 16)),
            dma((BATCHES,)),
            dma((BATCHES,)),
            dma((4,)),
            dma((4,)),
            dma,
            dma,
        ],
        compiler_params=pltpu.CompilerParams(
            collective_id=0, has_side_effects=True, vmem_limit_bytes=40 << 20
        ),
        name="step",
    )(*operands)
    return pl.pallas_call(
        finish_kernel,
        out_shape=(
            jax.ShapeDtypeStruct((1, rows, width), BF16),
            jax.ShapeDtypeStruct((1, rows), F32),
        ),
        in_specs=[pl.BlockSpec(memory_space=pltpu.VMEM)] * 3,
        out_specs=(pl.BlockSpec(memory_space=pl.ANY), pl.BlockSpec(memory_space=pltpu.VMEM)),
        scratch_shapes=[pltpu.VMEM((rows, HS), F32), dma],
        compiler_params=pltpu.CompilerParams(vmem_limit_bytes=16 << 20),
        name="loss",
    )(*held)


def solution(mesh):
    in_specs = (
        P(("segment", "fsdp"), "seq", None),
        P(("segment", "fsdp"), "seq"),
        P(("segment", "fsdp"), "seq", None),
        P("fsdp", None, None, None),
        P(),
        P(),
        P(),
        P(),
    )
    out_specs = (P(("segment", "fsdp"), "seq", None), P(("segment", "fsdp"), "seq"))
    return jax.shard_map(local, mesh=mesh, in_specs=in_specs, out_specs=out_specs, check_vma=False)
```

```python
import functools

import jax
import jax.numpy as jnp
from jax import lax
from jax.experimental import pallas as pl
from jax.experimental.pallas import tpu as pltpu
from jax.sharding import PartitionSpec as P

HS = 128
MESH = pl.DeviceIdType.MESH
F32 = jnp.float32
BF16 = jnp.bfloat16
HEADS_IN = (5, 8, 8, 8, 3)
BATCHES = len(HEADS_IN)
DIRECT = 3


def sigmoid(v):
    return 1.0 / (1.0 + jnp.exp(-v))


def minus_expm1(y, ey):
    series = 1.0 + y * (1 / 2 + y * (1 / 6 + y * (1 / 24 + y * (1 / 120 + y * (1 / 720)))))
    return jnp.where(y > -0.125, -y * series, 1.0 - ey)


def kernel(
    seq_len,
    x_hbm,
    pos_hbm,
    teach_hbm,
    gw_hbm,
    gb_hbm,
    cw_hbm,
    cb_hbm,
    rate_hbm,
    student,
    tbuf,
    norm_ref,
    x_v,
    halo,
    pos_v,
    gb_v,
    cw_v,
    cb_v,
    rate_v,
    wbuf,
    convb,
    prod_b,
    local_b,
    comp,
    rowc,
    allc,
    tot,
    ysum,
    inc_b,
    xf,
    masks,
    tmp,
    acc_b,
    load_sem,
    far_s,
    far_r,
    near_s,
    near_r,
    x_s,
    x_r,
    chip_s,
    chip_r,
    row_s,
    row_r,
    all_s,
    all_r,
    y_s,
    y_r,
    t_s,
    t_r,
    h_s,
    h_r,
):
    g, z, s = lax.axis_index("segment"), lax.axis_index("fsdp"), lax.axis_index("seq")
    planes, places = lax.axis_size("fsdp"), lax.axis_size("seq")
    row, here = s // 8, s % 8
    xc, core = here // 2, s % 2
    relay = lax.rem(z, 2) == core

    def at_z(dz):
        return (g, lax.rem(z + dz + planes, planes), s)

    def in_row(other):
        return (g, z, row * 8 + other)

    def remote(src, dst, send, recv, to):
        return pltpu.make_async_remote_copy(
            src_ref=src, dst_ref=dst, send_sem=send, recv_sem=recv, device_id=to, device_id_type=MESH
        )

    def await_bytes(ref, sem):
        pltpu.make_async_copy(ref, ref, sem).wait()

    loads = [
        pltpu.make_async_copy(gw_hbm.at[0], wbuf.at[0], load_sem.at[0]),
        pltpu.make_async_copy(x_hbm.at[0], x_v, load_sem.at[1]),
        pltpu.make_async_copy(pos_hbm, pos_v, load_sem.at[2]),
        pltpu.make_async_copy(cw_hbm, cw_v, load_sem.at[3]),
        pltpu.make_async_copy(cb_hbm, cb_v, load_sem.at[4]),
        pltpu.make_async_copy(gb_hbm, gb_v, load_sem.at[5]),
        pltpu.make_async_copy(rate_hbm, rate_v, load_sem.at[6]),
    ]
    for copy in loads:
        copy.start()

    partner = (1 - g, z, s)
    other_core = in_row(here // 2 * 2 + 1 - core)
    greeted = [at_z(dz) for dz in (8, -8, 4, -4, 3, -3, 2, -2, 1, -1)]
    greeted += [partner] + [(g, z, lax.rem(s + d, places)) for d in range(1, 16)]
    barrier = pltpu.get_barrier_semaphore()
    for device in greeted:
        pl.semaphore_signal(barrier, inc=1, device_id=device, device_id_type=MESH)
    loads[0].wait()
    pl.semaphore_wait(barrier, len(greeted))

    blocks = [pl.ds(32 * k, 32) for k in range(4)]
    quarter = pl.ds(pl.multiple_of(xc * 32, 32), 32)

    def span(j, kind):
        if j == 0:
            return kind, 2 if kind == 3 else 1
        return (32 + kind, 1) if j == 4 else (8 * j + 2 * kind, 2)

    def kinds(j, by_relay):
        if not by_relay:
            return (1, 2)
        return {0: (3,), 4: (0,)}.get(j, (0, 3))

    def piece(u, count):
        return wbuf.at[pl.ds(u, count), :, quarter, :]

    def far_copy(j, down):
        side = 1 if down else 0
        k = j - 1 + 4 * side
        dz = (4 if j % 2 else 8) * (-1 if down else 1)
        if j == 4:
            gate = pl.ds(side, 1)
            src, dst = (wbuf.at[pl.ds(u, 1), gate, quarter, :] for u in (16 + side, 32))
        else:
            src, dst = piece(16 + side if j == 3 else 0, 1), piece(8 * j + side, 1)
        return remote(src, dst, far_s.at[k], far_r.at[k], at_z(dz))

    def send_near(j):
        def send(u, count, kind, skip, dz, group=j):
            dst = piece(span(group, kind)[0] + skip, count)
            remote(piece(u, count), dst, near_s.at[j], near_r.at[kind, group], at_z(dz)).start()

        u, count = span(j, 0)
        above = u + count - 1
        if j == 3:
            send(above, 1, 1, 0, -3, 4)
            send(u, 1, 2, 0, 3, 4)
        send(u, 1, 3, 0, 2)
        send(above, 1, 3, 1, -2)
        send(u, count, 1, 0, 1)
        send(u, count, 2, 0, -1)

    def near_sent(j):
        return {0: wbuf.at[pl.ds(0, 1)], 3: wbuf.at[pl.ds(0, 2)]}.get(j, three(j, 0))

    def wait_near(j, kind):
        await_bytes(piece(*span(j, kind)), near_r.at[kind, j])

    def send_x(j, kind):
        src = piece(*span(j, kind))
        for d in (2, 1, 3):
            to = in_row(lax.rem(xc + d, 4) * 2 + core)
            remote(src, src, x_s.at[kind, j], x_r.at[kind, j], to).start()

    def three(j, kind):
        return wbuf.at[pl.ds(*span(j, kind)), :, pl.ds(0, 96), :]

    def chip_copy(j, kind):
        src = wbuf.at[pl.ds(*span(j, kind))]
        return remote(src, src, chip_s.at[kind, j], chip_r.at[kind, j], other_core)

    def both(for_relay, for_other):
        @pl.when(relay)
        def _():
            for_relay()

        @pl.when(jnp.logical_not(relay))
        def _():
            for_other()

    def far_copies(j):
        return [far_copy(j, down) for down in (False, True)]

    def start_far(j):
        for copy in far_copies(j):
            copy.start()

    def step_far(j):
        @pl.when(relay)
        def _():
            for copy in far_copies(j):
                copy.wait_recv()
            if j == 2:
                start_far(4)
                start_far(3)
            if j < 4:
                send_near(j)
            send_x(j, 0)

    def step_near(j):
        def get(by_relay):
            for kind in kinds(j, by_relay):
                if kind:
                    wait_near(j, kind)
                    send_x(j, kind)

        both(functools.partial(get, True), functools.partial(get, False))

    def step_x(j):
        def hand_over(by_relay):
            for kind in kinds(j, by_relay):
                await_bytes(three(j, kind), x_r.at[kind, j])
                chip_copy(j, kind).start()

        both(functools.partial(hand_over, True), functools.partial(hand_over, False))

    def step_chip(j):
        def get(by_relay):
            for kind in kinds(j, not by_relay):
                chip_copy(j, kind).wait_recv()

        both(functools.partial(get, True), functools.partial(get, False))

    @pl.when(relay)
    def _():
        start_far(2)
        start_far(1)
        send_near(0)

    halo_copy = remote(x_hbm.at[0, pl.ds(112, 16), :], halo, h_s, h_r, (g, z, lax.rem(s + 1, places)))
    teacher_copies = [
        remote(teach_hbm.at[0, block, :], tbuf.at[block, :], t_s.at[k], t_r.at[k], partner)
        for k, block in enumerate(blocks)
    ]

    @pl.when(s < places - 1)
    def _():
        halo_copy.start()

    for copy in teacher_copies:
        copy.start()
    for copy in loads[1:]:
        copy.wait()

    pos = jnp.transpose(jnp.broadcast_to(pos_v[...].astype(F32), (HS, HS)))
    tmp[...] = pos
    for v in range(16):
        places_v = tmp[pl.ds(v, 8, stride=16), :]
        for k in range(3):
            masks[k, pl.ds(8 * v, 8), :] = (places_v >= k + 1.0).astype(F32)
    comp[...] = jnp.zeros_like(comp)
    acc_b[...] = jnp.zeros_like(acc_b)

    def columns(head):
        return pl.ds(pl.multiple_of(head * HS, HS), HS)

    @pl.when(s > 0)
    def _():
        halo_copy.wait_recv()

    @pl.when(s == 0)
    def _():
        halo[...] = jnp.zeros_like(halo)

    def conv_head(head, _):
        cols = columns(head)
        xf[pl.ds(0, 16), :] = halo[:, cols].astype(F32)
        xf[pl.ds(16, HS), :] = x_v[:, cols].astype(F32)
        rows = {v: xf[pl.ds(16 + v, 8, stride=16), :] for v in range(-3, 16)}
        taps = [cw_v[pl.ds(k, 1), cols] for k in range(4)]
        bias = cb_v[:, cols]
        out = []
        for v in range(16):
            total = bias + taps[0] * rows[v]
            for k in range(1, 4):
                total = total + taps[k] * rows[v - k] * masks[k - 1, pl.ds(8 * v, 8), :]
            out.append(total)
        convb[head] = jnp.concatenate(out, axis=0).astype(BF16)
        return 0

    def head_of(j, index):
        if j in (0, 4):
            away = jnp.int32(0)
            for k, dz in enumerate((0, -1, 1, -2, 2) if j == 0 else (16, 15, -15)):
                away = jnp.where(index == k, dz, away)
        else:
            kind, side = index // 2, index % 2
            side = 2 * side - 1
            near = jnp.where(kind == 0, 0, jnp.where(kind == 1, -1, jnp.where(kind == 2, 1, 2 * side)))
            away = near + 4 * j * side
        return lax.rem(z + away + planes, planes)

    sub = lax.broadcasted_iota(jnp.int32, (8, HS), 0)

    def gates(j, index, _):
        u = 8 * j + index
        head = head_of(j, index)
        cols = columns(head)
        rows_b = convb[head]
        pre_x = jnp.dot(rows_b, wbuf[u, 0], preferred_element_type=F32)
        pre_a = jnp.dot(rows_b, wbuf[u, 1], preferred_element_type=F32)
        gate_x = sigmoid(pre_x + gb_v[pl.ds(0, 1), cols])
        gate_a = sigmoid(pre_a + gb_v[pl.ds(1, 1), cols])
        log_a = gate_a * (rate_v[:, cols] * (-8.0 / seq_len))
        keep = masks[0]
        decay = jnp.exp(log_a)
        scale = jnp.sqrt(minus_expm1(2.0 * log_a, decay * decay))
        scale = jnp.where(keep > 0.0, scale, 1.0)
        decay = decay * keep
        drive = rows_b.astype(F32) * gate_x * scale
        prods, states = [decay[0:8]], [drive[0:8]]
        for v in range(1, 16):
            step = decay[8 * v : 8 * v + 8]
            prods.append(prods[-1] * step)
            states.append(step * states[-1] + drive[8 * v : 8 * v + 8])
        p, q = prods[-1], states[-1]
        for d in (1, 2, 4):
            inside = sub >= d
            p_before = jnp.where(inside, pltpu.roll(p, d, 0), 1.0)
            q_before = jnp.where(inside, pltpu.roll(q, d, 0), 0.0)
            q = p * q_before + q
            p = p * p_before
        p_in = jnp.where(sub >= 1, pltpu.roll(p, 1, 0), 1.0)
        q_in = jnp.where(sub >= 1, pltpu.roll(q, 1, 0), 0.0)
        comp[0, pl.ds(u, 1), :] = p[7:8]
        comp[1, pl.ds(u, 1), :] = q[7:8]
        for v in range(16):
            prod_b[u, pl.ds(8 * v, 8), :] = prods[v] * p_in
            local_b[u, pl.ds(8 * v, 8), :] = states[v] + prods[v] * q_in
        return 0

    def compute(j):
        unroll = HEADS_IN[j] if HEADS_IN[j] < 8 else 4
        lax.fori_loop(0, HEADS_IN[j], functools.partial(gates, j), 0, unroll=unroll)

    def mine(j):
        return pl.ds(8 * j, 8)

    def send_row(j):
        rowc[here, :, mine(j), :] = comp[:, mine(j), :]
        src = comp.at[:, mine(j), :]
        for d in range(1, 8):
            to = in_row(lax.rem(here + d, 8))
            remote(src, rowc.at[here, :, mine(j), :], row_s.at[j], row_r.at[j], to).start()

    def direct_copy(j, d):
        k = j - DIRECT
        to = (g, z, lax.rem(s + d, places))
        return remote(comp.at[:, mine(j), :], allc.at[k, s], all_s.at[k, d - 1], all_r.at[k, s], to)

    def send_direct(j):
        for d in range(15, 0, -1):

            @pl.when(s + d < places)
            def _():
                direct_copy(j, d).start()

    def step_direct(j):
        c = j - DIRECT
        for k in range(15):

            @pl.when(k < s)
            def _():
                pltpu.make_async_copy(allc.at[c, k], allc.at[c, k], all_r.at[c, k]).wait()

        entering = jnp.zeros((8, HS), F32)
        for k in range(15):
            through = allc[c, k, 0] * entering + allc[c, k, 1]
            entering = jnp.where(k < s, through, entering)
        inc_b[1, mine(j), :] = entering
        finish_batch(j)

    def seven(j):
        return rowc.at[pl.ds(0, 7), :, mine(j), :]

    def y_copy(j):
        to = (g, z, lax.rem(s + 8, places))
        return remote(tot.at[mine(j)], ysum.at[mine(j)], y_s.at[j], y_r.at[j], to)

    def step_row(j):
        await_bytes(seven(j), row_r.at[j])
        all_p = jnp.zeros((8, HS), F32) + 1.0
        before_p, before_q, all_q = all_p, jnp.zeros((8, HS), F32), jnp.zeros((8, HS), F32)
        for k in range(8):
            a, b = rowc[k, 0, mine(j), :], rowc[k, 1, mine(j), :]
            before_p = jnp.where(k < here, before_p * a, before_p)
            before_q = jnp.where(k < here, a * before_q + b, before_q)
            all_q = a * all_q + b
        tot[mine(j), :] = all_q

        @pl.when(row == 0)
        def _():
            y_copy(j).start()

        inc_b[0, mine(j), :] = before_p
        inc_b[1, mine(j), :] = before_q

    def step_y(j):
        @pl.when(row == 1)
        def _():
            y_copy(j).wait_recv()
            inc_b[1, mine(j), :] = inc_b[0, mine(j), :] * ysum[mine(j), :] + inc_b[1, mine(j), :]

        finish_batch(j)

    def finish_batch(j):
        def finish(index, _):
            u = 8 * j + index
            cols = columns(head_of(j, index))
            entering = inc_b[1, pl.ds(u, 1), :]
            for v in range(16):
                full = local_b[u, pl.ds(8 * v, 8), :] + prod_b[u, pl.ds(8 * v, 8), :] * entering
                tmp[pl.ds(v, 8, stride=16), :] = full
            rounded = tmp[...].astype(BF16)
            student[:, cols] = rounded
            wide = rounded.astype(F32)
            acc_b[...] += wide * wide
            return 0

        unroll = HEADS_IN[j] if HEADS_IN[j] < 8 else 4
        lax.fori_loop(0, HEADS_IN[j], finish, 0, unroll=unroll)

    def sent(j):
        def clear(by_relay):
            if by_relay and j:
                for copy in far_copies(j):
                    copy.wait_send()
            if by_relay and j < 4:
                await_bytes(near_sent(j), near_s.at[j])
            for kind in kinds(j, by_relay):
                await_bytes(three(j, kind), x_s.at[kind, j])
                chip_copy(j, kind).wait_send()

        both(functools.partial(clear, True), functools.partial(clear, False))

    heads = x_v.shape[1] // HS
    lax.fori_loop(0, heads // 2, conv_head, 0, unroll=4)
    step_near(0)
    step_far(1)
    step_far(2)
    lax.fori_loop(heads // 2, heads, conv_head, 0, unroll=4)
    step_x(0)
    step_near(1)
    step_chip(0)
    compute(0)
    send_row(0)
    step_near(2)
    step_x(1)
    step_far(3)
    step_chip(1)
    compute(1)
    send_row(1)
    step_row(0)
    step_far(4)
    step_x(2)
    step_near(3)
    step_near(4)
    step_chip(2)
    compute(2)
    send_row(2)
    step_x(3)
    step_x(4)
    step_row(1)
    step_y(0)
    step_chip(3)
    compute(3)
    send_direct(3)
    step_chip(4)
    compute(4)
    send_direct(4)
    step_row(2)
    step_y(1)
    for j in range(BATCHES):
        sent(j)
    step_y(2)
    step_direct(3)
    step_direct(4)

    mean_sq = jnp.sum(acc_b[...], axis=1, keepdims=True) * (1.0 / x_v.shape[1])
    norm_ref[...] = jnp.broadcast_to(lax.rsqrt(mean_sq + 1e-06), (HS, HS))
    for copy in teacher_copies:
        copy.wait_recv()

    for copy in teacher_copies:
        copy.wait_send()

    @pl.when(s < places - 1)
    def _():
        halo_copy.wait_send()

    @pl.when(row == 0)
    def _():
        for j in range(DIRECT):
            y_copy(j).wait_send()

    for j in range(DIRECT):
        await_bytes(seven(j), row_s.at[j])
    for d in range(1, 16):

        @pl.when(s + d < places)
        def _():
            for j in range(DIRECT, BATCHES):
                direct_copy(j, d).wait_send()


def finish_kernel(student, target, norm_ref, out_hbm, loss_ref, acc_b, out_sem):
    out_copy = pltpu.make_async_copy(student, out_hbm.at[0], out_sem)
    out_copy.start()
    width = student.shape[1]
    for k in range(4):
        block = pl.ds(32 * k, 32)

        def loss_head(head, total):
            cols = pl.ds(pl.multiple_of(head * HS, HS), HS)
            diff = student[block, cols].astype(F32) * norm_ref[block, :] - target[block, cols].astype(F32)
            return total + diff * diff

        zero = jnp.zeros((32, HS), F32)
        acc_b[block, :] = lax.fori_loop(0, width // HS, loss_head, zero, unroll=8)
    loss_ref[...] = jnp.sum(jnp.transpose(acc_b[...]), axis=0, keepdims=True) * (1.0 / width)
    out_copy.wait()


def local(branch_x, positions, teacher, gate_weights, gate_bias, conv_weight, conv_bias, decay_rate):
    rows, width = branch_x.shape[1:]
    seq_len = rows * lax.axis_size("seq")
    slots = 8 * BATCHES
    dma = pltpu.SemaphoreType.DMA
    operands = (
        branch_x,
        positions,
        teacher,
        gate_weights,
        gate_bias,
        conv_weight,
        conv_bias.reshape(1, width),
        decay_rate.reshape(1, width),
    )
    operands = [pltpu.with_memory_space_constraint(v, pltpu.HBM) for v in operands]
    held = pl.pallas_call(
        functools.partial(kernel, seq_len),
        out_shape=(
            jax.ShapeDtypeStruct((rows, width), BF16),
            jax.ShapeDtypeStruct((rows, width), BF16),
            jax.ShapeDtypeStruct((rows, HS), F32),
        ),
        in_specs=[pl.BlockSpec(memory_space=pltpu.HBM)] * 8,
        out_specs=[pl.BlockSpec(memory_space=pltpu.VMEM)] * 3,
        scratch_shapes=[
            pltpu.VMEM((rows, width), BF16),
            pltpu.VMEM((16, width), BF16),
            pltpu.VMEM((1, rows), jnp.int32),
            pltpu.VMEM((2, width), F32),
            pltpu.VMEM((4, width), F32),
            pltpu.VMEM((1, width), F32),
            pltpu.VMEM((1, width), F32),
            pltpu.VMEM((slots, 2, HS, HS), BF16),
            pltpu.VMEM((width // HS, rows, HS), BF16),
            pltpu.VMEM((slots, rows, HS), F32),
            pltpu.VMEM((slots, rows, HS), F32),
            pltpu.VMEM((2, slots, HS), F32),
            pltpu.VMEM((8, 2, slots, HS), F32),
            pltpu.VMEM((BATCHES - DIRECT, 16, 2, 8, HS), F32),
            pltpu.VMEM((slots, HS), F32),
            pltpu.VMEM((slots, HS), F32),
            pltpu.VMEM((2, slots, HS), F32),
            pltpu.VMEM((rows + 16, HS), F32),
            pltpu.VMEM((3, rows, HS), F32),
            pltpu.VMEM((rows, HS), F32),
            pltpu.VMEM((rows, HS), F32),
            dma((7,)),
            dma((8,)),
            dma((8,)),
            dma((BATCHES,)),
            dma((4, BATCHES)),
            dma((4, BATCHES)),
            dma((4, BATCHES)),
            dma((4, BATCHES)),
            dma((4, BATCHES)),
            dma((BATCHES,)),
            dma((BATCHES,)),
            dma((BATCHES - DIRECT, 15)),
            dma((BATCHES - DIRECT, 16)),
            dma((BATCHES,)),
            dma((BATCHES,)),
            dma((4,)),
            dma((4,)),
            dma,
            dma,
        ],
        compiler_params=pltpu.CompilerParams(
            collective_id=0, has_side_effects=True, vmem_limit_bytes=40 << 20
        ),
        name="step",
    )(*operands)
    return pl.pallas_call(
        finish_kernel,
        out_shape=(
            jax.ShapeDtypeStruct((1, rows, width), BF16),
            jax.ShapeDtypeStruct((1, rows), F32),
        ),
        in_specs=[pl.BlockSpec(memory_space=pltpu.VMEM)] * 3,
        out_specs=(pl.BlockSpec(memory_space=pl.ANY), pl.BlockSpec(memory_space=pltpu.VMEM)),
        scratch_shapes=[pltpu.VMEM((rows, HS), F32), dma],
        compiler_params=pltpu.CompilerParams(vmem_limit_bytes=16 << 20),
        name="loss",
    )(*held)


def solution(mesh):
    in_specs = (
        P(("segment", "fsdp"), "seq", None),
        P(("segment", "fsdp"), "seq"),
        P(("segment", "fsdp"), "seq", None),
        P("fsdp", None, None, None),
        P(),
        P(),
        P(),
        P(),
    )
    out_specs = (P(("segment", "fsdp"), "seq", None), P(("segment", "fsdp"), "seq"))
    return jax.shard_map(local, mesh=mesh, in_specs=in_specs, out_specs=out_specs, check_vma=False)
```
